32 devices in a mesh: tgt: 4 (over y, core), blk: 8 (over z, x).
Axes of the slice: x: 2, y: 2, z: 4, core: 2. Of those that a mesh axis runs over, the one named last changes fastest.
Arguments:
- integrals: bfloat16 [8192, 128, 128], P(('tgt', 'blk')), may hold values from -0.5 to 0.5
- densities: bfloat16 [60, 128, 128], P('tgt'), may hold values from -1.5 to 1.5
- entry_block: int32 [65536], P(('tgt', 'blk')), may hold values from 0 to 255
- entry_state: int32 [65536], P(('tgt', 'blk')), may hold values from 0 to 59, as said below
- entry_slot: int32 [65536], P(('tgt', 'blk')), may hold values from 0 to 127
- counts: int32 [32, 4], P(('tgt', 'blk')), may hold values from 0 to 2048, as said below
- owner: int32 [1024], P('blk'), may hold values from 0 to 1023, as said below
Outputs:
- hamiltonian: float32 [1024, 128, 128], P(('tgt', 'blk'))
The draws below stay inside these ranges and needn't reach their ends.
Inputs may be any that keep to these rules, and one draw needn't show every extreme that they name: `counts`: each row sums to at most 2048; on some device all 2048 slots are live and belong to a single group of target states. `entry_state`: within each device's slots, the first counts[d, 0] name states of group 0 (states 0 to 14), the next counts[d, 1] states of group 1, and so on; the slots after the live ones are unused. `owner`: A permutation of 0 to 1023; output positions d * 32 to (d + 1) * 32 - 1 belong to device d, and of the 128 blocks of one block-row group exactly 4 go to each device.
All inputs are finite; a program needn't handle non-finite values.
Results may differ from the reference program's by a relative error of at most 0.0003.
Values may be sent and summed in bfloat16 or wider, within the bound.
A program may use at most 128 MiB of HBM per device.

```python
import jax
import jax.numpy as jnp
from jax import lax

BS = 128
STATES = 60
E_CAP = 2048
G_DEV = 256
HB_DEV = 128
SHARDS = 4
BLOCK_GROUPS = 8
S_DEV = 15
NH = 1024
OWN_DEV = 32
PER_DEV = 4
N_BLK = 8
DEVICES = 32


def segment_counts(key):
    ndev = SHARDS * BLOCK_GROUPS
    key_a, key_b, key_c, key_d, key_e = jax.random.split(key, 5)
    totals = jax.random.randint(key_a, (ndev,), E_CAP // 8, E_CAP // 2 + 1)
    packed = jax.random.randint(key_b, (ndev,), 0, 8) == 0
    forced = jnp.arange(ndev) == jax.random.randint(key_c, (), 0, ndev)
    totals = jnp.where(packed | forced, E_CAP, totals).astype(jnp.int32)
    cuts = jnp.sort(jax.random.randint(key_d, (ndev, SHARDS - 1), 0, E_CAP + 1), axis=1)
    chosen = jax.random.randint(key_e, (), 0, SHARDS)
    single = jnp.where(jnp.arange(SHARDS - 1) < chosen, 0, E_CAP).astype(jnp.int32)
    cuts = jnp.where(forced[:, None], single[None, :], cuts)
    cuts = cuts * totals[:, None] // E_CAP
    edges = jnp.concatenate([jnp.zeros((ndev, 1), jnp.int32), cuts.astype(jnp.int32), totals[:, None]], axis=1)
    return jnp.diff(edges, axis=1).astype(jnp.int32)


def draw_counts(key, part):
    return segment_counts(jax.random.fold_in(key, 11))


def draw_entry_state(key, part):
    counts = segment_counts(jax.random.fold_in(key, 11))
    ndev = SHARDS * BLOCK_GROUPS
    ends = jnp.cumsum(counts, axis=1)
    pos = jnp.arange(E_CAP, dtype=jnp.int32)
    group = jnp.sum((pos[None, :, None] >= ends[:, None, :SHARDS - 1]).astype(jnp.int32), axis=2)
    live = pos[None, :] < ends[:, -1:]
    key_a, key_b = jax.random.split(jax.random.fold_in(key, 23))
    spare = jax.random.randint(key_a, (ndev, E_CAP), 0, SHARDS)
    group = jnp.where(live, group, spare)
    inner = jax.random.randint(key_b, (ndev, E_CAP), 0, S_DEV)
    return (group * S_DEV + inner).astype(jnp.int32).reshape(-1)


def draw_owner(key, part):
    key_a, key_b = jax.random.split(jax.random.fold_in(key, 37))
    ndev = SHARDS * BLOCK_GROUPS
    source_keys = jax.random.split(key_a, BLOCK_GROUPS)
    dest = jax.vmap(lambda k: jax.random.permutation(k, HB_DEV))(source_keys).astype(jnp.int32)
    device = dest // PER_DEV
    within = dest % PER_DEV
    before = jnp.arange(BLOCK_GROUPS, dtype=jnp.int32)[:, None] * PER_DEV + within
    device_keys = jax.random.split(key_b, ndev)
    shuffle = jax.vmap(lambda k: jax.random.permutation(k, OWN_DEV))(device_keys).astype(jnp.int32)
    local = shuffle[device, before]
    return (device * OWN_DEV + local).astype(jnp.int32).reshape(-1)


def plant(array, key, smallest, high):
    shape = array.shape
    index_at = [jax.random.randint(jax.random.fold_in(key, axis), (), 0, shape[axis]) for axis in range(len(shape))]
    array = array.at[tuple(index_at)].set(smallest)
    longest = shape.index(max(shape))
    index_at[longest] = (index_at[longest] + 1) % shape[longest]
    return array.at[tuple(index_at)].set(high)


def levels(own_key, extent, shards, low, top_value):
    loudness, own = 1.0, jax.random.fold_in(own_key, 6)
    for dim, shards_of in shards:
        heights = jnp.exp(jax.random.uniform(jax.random.fold_in(own, dim), (shards_of,), jnp.float32, low / len(shards), top_value / len(shards)))
        loudness = loudness * jnp.repeat(heights, extent[dim] // shards_of).reshape([-1 if axis == dim else 1 for axis in range(len(extent))])
    return loudness


def noise(key, dims, scale, limit, pieces=(), held_as=jnp.bfloat16):
    array = scale * jax.random.normal(key, dims, jnp.float32)
    if pieces:
        array = array * levels(key, dims, pieces, -0.22, 0.18)
    return jnp.clip(array, -limit, limit).astype(held_as)


def setup_inputs(seed: int = 0) -> dict:
    keys = jax.random.split(jax.random.key(seed), 8)
    integrals = noise(keys[0], (DEVICES * G_DEV, BS, BS), BS ** -0.5, 0.5, ((0, 32),))
    densities = noise(keys[1], (STATES, BS, BS), 0.25, 1.5, ((0, 4),))
    entry_block = plant(jax.random.randint(keys[2], (DEVICES * E_CAP,), 0, G_DEV), jax.random.fold_in(keys[2], 1), 0, G_DEV - 1).astype(jnp.int32)
    entry_state = draw_entry_state(jax.random.fold_in(keys[7], 71), 0)
    entry_slot = plant(jax.random.randint(keys[4], (DEVICES * E_CAP,), 0, HB_DEV), jax.random.fold_in(keys[4], 1), 0, HB_DEV - 1).astype(jnp.int32)
    counts = draw_counts(jax.random.fold_in(keys[7], 71), 0)
    owner = draw_owner(jax.random.fold_in(keys[7], 71), 0)
    return {"integrals": integrals, "densities": densities, "entry_block": entry_block, "entry_state": entry_state, "entry_slot": entry_slot, "counts": counts, "owner": owner}


def reference(integrals, densities, entry_block, entry_state, entry_slot, counts, owner):
    devices = counts.shape[0]
    width = min(128, E_CAP)
    blocks = entry_block.reshape(devices, E_CAP)
    states = entry_state.reshape(devices, E_CAP)
    slots = entry_slot.reshape(devices, E_CAP)
    totals = jnp.sum(counts, axis=1).astype(jnp.int32)
    flat = BS * BS

    def per_device(full, dev):
        local = lax.dynamic_slice_in_dim(integrals, (dev * G_DEV).astype(jnp.int32), G_DEV, 0)
        live_total = totals[dev]
        steps = (live_total + width - 1) // width

        def group(j, acc):
            begin = (j * width).astype(jnp.int32)
            pos = begin + jnp.arange(width, dtype=jnp.int32)
            valid = pos < live_total
            blk_ids = lax.dynamic_slice_in_dim(blocks[dev], begin, width)
            st_ids = lax.dynamic_slice_in_dim(states[dev], begin, width)
            sl_ids = lax.dynamic_slice_in_dim(slots[dev], begin, width)
            left = local[blk_ids].astype(jnp.float32)
            right = densities[st_ids].astype(jnp.float32)
            prod = jnp.einsum("ekm,emn->ekn", left, right)
            prod = jnp.where(valid[:, None, None], prod, jnp.zeros_like(prod))
            return acc.at[sl_ids].add(prod.reshape(width, flat))

        partial_value = lax.fori_loop(0, steps, group, jnp.zeros((HB_DEV, flat), jnp.float32))
        row = ((dev % N_BLK) * HB_DEV).astype(jnp.int32)
        current = lax.dynamic_slice_in_dim(full, row, HB_DEV, 0)
        full = lax.dynamic_update_slice_in_dim(full, current + partial_value, row, 0)
        return full, None

    full, _ = lax.scan(per_device, jnp.zeros((NH, flat), jnp.float32), jnp.arange(devices, dtype=jnp.int32))
    placed = jnp.zeros_like(full).at[owner].set(full)
    return placed.reshape(NH, BS, BS)
```

```python
import jax
import jax.numpy as jnp
from jax import lax
from jax.experimental import pallas as pl
from jax.experimental.pallas import tpu as pltpu
from jax.sharding import PartitionSpec as P

CAP = 16
CHUNK = 4
UNROLL = 16
STEPS = 8
LAG = 2
PIECES = 3
LANES = 128
MESH = pl.DeviceIdType.MESH
LEVELS = 32767.0
SMALLEST = 1e-33


def route(entry_block, entry_state, entry_slot, counts, owner, integrals, densities, own_rows):
    s_group, size, _ = densities.shape
    states = s_group * lax.axis_size("tgt")
    half = size // 2
    cut = s_group // PIECES
    e_cap = entry_block.shape[0]
    hb_rows = owner.shape[0]
    groups = e_cap // LANES
    flat = (groups, LANES)
    fixed = hb_rows * CAP
    tall = (fixed + e_cap) // LANES

    def kernel(counts_ref, block_hbm, state_hbm, slot_hbm, owner_hbm, int_hbm, den_hbm,
               keys_ref, pos_ref, ints_ref, table_ref, block_ref, state_ref, slot_ref, owner_ref,
               hot, pre, left, right, sems, y_send, y_recv, x_send, x_recv, c_send, c_recv,
               o_send, o_recv):
        t = lax.axis_index("tgt")
        b = lax.axis_index("blk")
        beside = (t // 2) * 2 + 1 - t % 2
        across = (1 - t // 2) * 2 + t % 2
        beyond = (1 - t // 2) * 2 + 1 - t % 2
        mate = (b // 2) * 2 + 1 - b % 2
        side = b % 2

        def part(group, p, which):
            return table_ref.at[
                pl.ds(1 + group * s_group + p * cut, cut), pl.ds(which * half, half)
            ]

        def over_y(p, to):
            return pltpu.make_async_remote_copy(
                src_ref=den_hbm.at[pl.ds(p * cut, cut), pl.ds(side * half, half)],
                dst_ref=part(to, p, side),
                send_sem=y_send.at[p], recv_sem=y_recv.at[p],
                device_id={"tgt": across}, device_id_type=MESH,
            )

        def over_x(p, which):
            return pltpu.make_async_remote_copy(
                src_ref=part(across, p, which), dst_ref=part(across, p, which),
                send_sem=x_send.at[p], recv_sem=x_recv.at[p],
                device_id={"blk": mate}, device_id_type=MESH,
            )

        def pass_on(group, p, which, i):
            return pltpu.make_async_remote_copy(
                src_ref=part(group, p, which), dst_ref=part(group, p, which),
                send_sem=c_send.at[i, p], recv_sem=c_recv.at[i, p],
                device_id={"tgt": beside}, device_id_type=MESH,
            )

        def share(group):
            return pltpu.make_async_remote_copy(
                src_ref=den_hbm, dst_ref=table_ref.at[pl.ds(1 + group * s_group, s_group)],
                send_sem=o_send, recv_sem=o_recv,
                device_id={"tgt": beside}, device_id_type=MESH,
            )

        barrier = pltpu.get_barrier_semaphore()
        for peer in ({"tgt": beside}, {"tgt": across}, {"blk": mate}):
            pl.semaphore_signal(barrier, inc=1, device_id=peer, device_id_type=MESH)
        moves = (
            (slot_hbm, slot_ref), (owner_hbm, owner_ref), (block_hbm, block_ref),
            (state_hbm, state_ref), (int_hbm, ints_ref),
            (den_hbm, table_ref.at[pl.ds(1 + t * s_group, s_group)]),
        )
        loads = [
            pltpu.make_async_copy(src, dst, sems.at[i]) for i, (src, dst) in enumerate(moves)
        ]
        for load in loads:
            load.start()
        table_ref[0] = jnp.zeros((size, size), table_ref.dtype)
        pl.semaphore_wait(barrier, 3)
        for p in range(PIECES):
            over_y(p, t).start()
        share(t).start()
        live = counts_ref[0, 0]
        for i in range(1, counts.shape[1]):
            live = live + counts_ref[0, i]
        lane = lax.broadcasted_iota(jnp.int32, (1, LANES), 1)
        sub = lax.broadcasted_iota(jnp.int32, (hb_rows, LANES), 0)
        wide = lax.broadcasted_iota(jnp.int32, (hb_rows, LANES), 1)
        loads[0].wait()
        for g in range(groups):
            ok = g * LANES + lane < live
            slot = jnp.where(ok, slot_ref[g:g + 1, :], -1)
            hot[g * hb_rows:(g + 1) * hb_rows, :] = jnp.where(
                sub == slot, 1.0, 0.0
            ).astype(jnp.bfloat16)
        before = jnp.where(sub < wide, 1.0, 0.0).astype(jnp.bfloat16)
        after = jnp.where(wide < sub, 1.0, 0.0).astype(jnp.bfloat16)
        ones = jnp.ones((LANES, LANES), jnp.bfloat16)
        counted = jnp.dot(
            hot[...], jnp.concatenate([before, ones], axis=1), preferred_element_type=jnp.float32
        )
        running = jnp.zeros((hb_rows, LANES), jnp.float32)
        for g in range(groups):
            piece = counted[g * hb_rows:(g + 1) * hb_rows]
            pre[g] = piece[:, :LANES] + running
            running = running + piece[:, LANES:]
        for load in loads[1:4]:
            load.wait()
        mine = jnp.broadcast_to(owner_ref[...], (hb_rows, LANES))
        column = jnp.transpose(mine)
        smaller = jnp.where(mine < column, 1.0, 0.0).astype(jnp.bfloat16)
        place = jnp.dot(smaller, ones, preferred_element_type=jnp.float32)
        local = (column % own_rows).astype(jnp.float32)
        pos_ref[0] = jnp.sum(
            jnp.where(place.astype(jnp.int32) == wide, local, 0.0), axis=0, keepdims=True
        ).astype(jnp.int32)
        chunks = jnp.floor((jnp.maximum(running - CAP, 0.0) + (CHUNK - 1)) * (1.0 / CHUNK))
        high = jnp.floor(chunks * (1.0 / 16))
        low = chunks - 16 * high
        start = 16 * jnp.dot(
            after, high.astype(jnp.bfloat16), preferred_element_type=jnp.float32
        ) + jnp.dot(after, low.astype(jnp.bfloat16), preferred_element_type=jnp.float32)
        total = start[hb_rows - 1:, :] + chunks[hb_rows - 1:, :]
        base_fixed = place * CAP
        base_rest = start * CHUNK + (fixed - CAP)
        tall_sub = lax.broadcasted_iota(jnp.int32, (tall, LANES), 0)
        for g in range(groups):
            at = slice(g * LANES, (g + 1) * LANES)
            here = hot[g * hb_rows:(g + 1) * hb_rows, :].astype(jnp.float32)
            seen = pre[g]
            goal = seen + jnp.where(seen < CAP, base_fixed, base_rest)
            goal = jnp.sum(goal * here, axis=0, keepdims=True).astype(jnp.int32)
            row = jnp.sum(place * here, axis=0, keepdims=True)
            ok = g * LANES + lane < live
            goal = jnp.where(ok, goal, -1)
            left[:, at] = jnp.where(tall_sub == goal // LANES, 1.0, 0.0).astype(jnp.bfloat16)
            match = sub == goal % LANES
            digits = (
                block_ref[g:g + 1, :].astype(jnp.float32),
                (state_ref[g:g + 1, :] + 1).astype(jnp.float32),
                row,
            )
            for d, digit in enumerate(digits):
                right[d * LANES:(d + 1) * LANES, at] = jnp.where(match, digit, 0.0).astype(
                    jnp.bfloat16
                )
        table = lax.dot_general(
            left[...], right[...], (((1,), (1,)), ((), ())), preferred_element_type=jnp.float32
        ).astype(jnp.int32)
        keys_ref[:tall] = (
            table[:, :LANES] + (table[:, LANES:2 * LANES] << 8) + (table[:, 2 * LANES:] << 16)
        )
        keys_ref[tall:] = jnp.broadcast_to(total, (8, LANES)).astype(jnp.int32)
        for p in range(PIECES):
            over_y(p, across).wait_recv()
            over_x(p, side).start()
            pass_on(across, p, side, 0).start()
        for p in range(PIECES):
            over_x(p, 1 - side).wait_recv()
            pass_on(across, p, 1 - side, 1).start()
        share(beside).wait_recv()
        for p in range(PIECES):
            pass_on(beyond, p, side, 0).wait_recv()
            pass_on(beyond, p, 1 - side, 1).wait_recv()
        for p in range(PIECES):
            over_y(p, t).wait_send()
            over_x(p, side).wait_send()
            pass_on(across, p, side, 0).wait_send()
            pass_on(across, p, 1 - side, 1).wait_send()
        share(t).wait_send()
        loads[4].wait()
        loads[5].wait()

    vmem = pl.BlockSpec(memory_space=pltpu.VMEM)
    dma = pltpu.SemaphoreType.DMA
    return pl.pallas_call(
        kernel,
        out_shape=(
            jax.ShapeDtypeStruct((tall + 8, LANES), jnp.int32),
            jax.ShapeDtypeStruct((1, 1, LANES), jnp.int32),
            jax.ShapeDtypeStruct(integrals.shape, integrals.dtype),
            jax.ShapeDtypeStruct((states + 1, size, size), densities.dtype),
        ),
        in_specs=[pl.BlockSpec(memory_space=pltpu.SMEM)]
        + [pl.BlockSpec(memory_space=pl.ANY)] * 6,
        out_specs=(vmem,) * 4,
        scratch_shapes=[
            pltpu.VMEM(flat, jnp.int32),
            pltpu.VMEM(flat, jnp.int32),
            pltpu.VMEM(flat, jnp.int32),
            pltpu.VMEM((1, hb_rows), jnp.int32),
            pltpu.VMEM((groups * hb_rows, LANES), jnp.bfloat16),
            pltpu.VMEM((groups, hb_rows, LANES), jnp.float32),
            pltpu.VMEM((tall, e_cap), jnp.bfloat16),
            pltpu.VMEM((3 * LANES, e_cap), jnp.bfloat16),
            dma((6,)),
            dma((PIECES,)), dma((PIECES,)), dma((PIECES,)), dma((PIECES,)),
            dma((2, PIECES)), dma((2, PIECES)), dma, dma,
        ],
        compiler_params=pltpu.CompilerParams(
            collective_id=1, has_side_effects=True, vmem_limit_bytes=38 << 20
        ),
    )(
        counts, entry_block.reshape(flat), entry_state.reshape(flat), entry_slot.reshape(flat),
        owner.reshape(1, hb_rows), integrals, densities,
    )


def spill(keys, integrals, table, hb_rows):
    size = table.shape[-1]
    fixed = hb_rows * CAP
    tall = keys.shape[0] - 8

    def kernel(keys_ref, ints, dens, acc):
        @pl.loop(0, hb_rows)
        def _(j):
            acc[j] = jnp.zeros((size, size), jnp.float32)

        @pl.loop(0, (keys_ref[tall, 0] + UNROLL - 1) // UNROLL)
        def _(step):
            prods = []
            for u in range(UNROLL):
                base = fixed + (step * UNROLL + u) * CHUNK
                ks = [keys_ref[(base + i) >> 7, (base + i) & 127] for i in range(CHUNK)]
                lhs = jnp.concatenate([ints[k & 255] for k in ks], axis=1)
                rhs = jnp.concatenate([dens[(k >> 8) & 255] for k in ks], axis=0)
                prods.append(
                    (ks[0] >> 16, jnp.dot(lhs, rhs, preferred_element_type=jnp.float32))
                )
            for row, prod in prods:
                acc[row] += prod

    vmem = pl.BlockSpec(memory_space=pltpu.VMEM)
    return pl.pallas_call(
        kernel,
        out_shape=jax.ShapeDtypeStruct((hb_rows, size, size), jnp.float32),
        in_specs=[pl.BlockSpec(memory_space=pltpu.SMEM), vmem, vmem],
        out_specs=vmem,
        compiler_params=pltpu.CompilerParams(vmem_limit_bytes=8 << 20),
    )(keys, integrals, table)


def narrow(x):
    top = jnp.maximum(jnp.max(jnp.abs(x), axis=0, keepdims=True), SMALLEST)
    return jnp.round(x * (LEVELS / top)).astype(jnp.int32).astype(jnp.int16), top * (1.0 / LEVELS)


def widen(q, step):
    return q.astype(jnp.int32).astype(jnp.float32) * step


def exchange(keys, integrals, table, extra, pos, own_rows, n_blk):
    size = integrals.shape[-1]
    steps = min(STEPS, n_blk)
    rows = own_rows // steps
    dests = n_blk // steps
    per = own_rows // n_blk
    hb_rows = extra.shape[0]

    def kernel(keys_ref, ints, dens, base, pos_ref, out, pos_out, acc, r1, s2, r2, s3, got,
               step2, step2_in, step3, step3_in, s1_send, s1_recv, s2_send, s2_recv, t2_send,
               t2_recv, s3_send, s3_recv, t3_send, t3_recv, p_send, p_recv):
        t = lax.axis_index("tgt")
        b = lax.axis_index("blk")
        y, c = t // 2, t % 2
        sibling = y * 2 + (1 - c)
        across = (1 - y) * 2 + c
        barrier = pltpu.get_barrier_semaphore()
        pl.semaphore_signal(barrier, inc=1, device_id={"tgt": sibling}, device_id_type=MESH)
        pl.semaphore_signal(barrier, inc=1, device_id={"tgt": across}, device_id_type=MESH)
        for i in range(1, n_blk):
            pl.semaphore_signal(
                barrier, inc=1, device_id={"blk": (b + i) % n_blk}, device_id_type=MESH
            )

        def shift(i):
            return steps // 2 + (1 - 2 * (i % 2)) * ((i + 1) // 2)

        def line(i):
            return (b // dests + shift(i)) % steps

        def span(i):
            return line(i) * rows

        def first(i, far):
            side = 1 - y if far else y
            return pltpu.make_async_remote_copy(
                src_ref=acc.at[pl.ds((side * 2 + 1 - c) * own_rows + span(i), rows)],
                dst_ref=r1.at[far, pl.ds(span(i), rows)],
                send_sem=s1_send.at[far, i],
                recv_sem=s1_recv.at[far, i],
                device_id={"tgt": sibling},
                device_id_type=MESH,
            )

        def second(i):
            return pltpu.make_async_remote_copy(
                src_ref=s2.at[pl.ds(span(i), rows)],
                dst_ref=r2.at[pl.ds(span(i), rows)],
                send_sem=s2_send.at[i],
                recv_sem=s2_recv.at[i],
                device_id={"tgt": across},
                device_id_type=MESH,
            )

        def second_steps(i):
            return pltpu.make_async_remote_copy(
                src_ref=step2.at[i],
                dst_ref=step2_in.at[i],
                send_sem=t2_send.at[i],
                recv_sem=t2_recv.at[i],
                device_id={"tgt": across},
                device_id_type=MESH,
            )

        def third(dest, slot):
            return pltpu.make_async_remote_copy(
                src_ref=s3.at[pl.ds(dest * per, per)],
                dst_ref=got.at[pl.ds(slot * per, per)],
                send_sem=s3_send.at[dest],
                recv_sem=s3_recv.at[slot],
                device_id={"blk": dest},
                device_id_type=MESH,
            )

        def third_steps(dest, slot):
            return pltpu.make_async_remote_copy(
                src_ref=step3.at[dest],
                dst_ref=step3_in.at[slot],
                send_sem=t3_send.at[dest],
                recv_sem=t3_recv.at[slot],
                device_id={"blk": dest},
                device_id_type=MESH,
            )

        def places(dest, slot):
            return pltpu.make_async_remote_copy(
                src_ref=pos_ref.at[0],
                dst_ref=pos_out.at[slot],
                send_sem=p_send.at[dest],
                recv_sem=p_recv.at[slot],
                device_id={"blk": dest},
                device_id_type=MESH,
            )

        def multiply(i, far):
            side = 1 - y if far else y
            for core in (1 - c, c):
                for k in range(rows):
                    row = (side * 2 + core) * own_rows + span(i) + k
                    ks = []
                    for e in range(CAP):
                        at = row * CAP + e
                        ks.append(keys_ref[at // LANES, at % LANES])
                    lhs = jnp.concatenate([ints[key & 255] for key in ks], axis=1)
                    rhs = jnp.concatenate([dens[(key >> 8) & 255] for key in ks], axis=0)
                    acc[row] = base[row] + jnp.dot(lhs, rhs, preferred_element_type=jnp.float32)

        def reduce_far(i):
            for k in range(rows):
                row = span(i) + k
                q, step = narrow(acc[((1 - y) * 2 + c) * own_rows + row] + r1[1, row])
                s2[row] = q
                step2[i, k:k + 1, :] = step
            for k in range(rows, 8):
                step2[i, k:k + 1, :] = jnp.zeros((1, size), jnp.float32)

        def dest_of(i, j):
            return line(i) * dests + (b % dests + j) % dests

        def reduce_near(i, own):
            for j in range(dests):
                dest = dest_of(i, j)
                for k in range(per):
                    row = dest * per + k
                    at = (b % dests + j) % dests * per + k if dests > 1 else k
                    scale = step2_in[i, pl.ds(at, 1), :]
                    total = acc[(y * 2 + c) * own_rows + row] + r1[0, row] + widen(r2[row], scale)
                    if own and j == 0:
                        out[row] = total
                    else:
                        q, step = narrow(total)
                        s3[row] = q
                        step3[dest, k:k + 1, :] = step
                for k in range(per, 8):
                    step3[dest, k:k + 1, :] = jnp.zeros((1, size), jnp.float32)

        def await_near(i):
            first(i, 0).wait_recv()
            second(i).wait_recv()
            second_steps(i).wait_recv()

        def send_far(i):
            second(i).start()
            second_steps(i).start()

        def send_near(i, own):
            for j in range(1 if own else 0, dests):
                dest = dest_of(i, j)
                third(dest, b).start()
                third_steps(dest, b).start()

        multiply(0, 1)
        pl.semaphore_wait(barrier, n_blk + 1)
        first(0, 1).start()
        for i in range(1, n_blk):
            places((b + i) % n_blk, b).start()
        pos_out[b] = pos_ref[0]
        multiply(0, 0)
        first(0, 0).start()

        def turn(i, carry, late):
            first(i - 1, 1).wait_recv()
            multiply(i, 1)
            reduce_far(i - 1)
            first(i, 1).start()
            send_far(i - 1)
            if late:
                await_near(i - LAG)
            multiply(i, 0)
            if late:
                reduce_near(i - LAG, False)
            first(i, 0).start()
            if late:
                send_near(i - LAG, False)
            return carry

        lax.fori_loop(1, LAG, lambda i, v: turn(i, v, False), 0)
        lax.fori_loop(LAG, steps, lambda i, v: turn(i, v, True), 0)
        first(steps - 1, 1).wait_recv()
        reduce_far(steps - 1)
        send_far(steps - 1)
        for i in range(steps - LAG, steps):
            own = i == steps - 1
            await_near(i)
            reduce_near(i, own)
            send_near(i, own)

        def arrive(i, carry):
            for j in range(dests):
                source = (b // dests - shift(i) + steps) % steps * dests
                source = source + (b % dests - j + dests) % dests
                third(source, source).wait_recv()
                third_steps(source, source).wait_recv()
                for k in range(per):
                    out[source * per + k] = widen(
                        got[source * per + k], step3_in[source, k:k + 1, :]
                    )
            return carry

        lax.fori_loop(0, steps - 1, arrive, 0)
        for j in range(1, dests):
            source = b // dests * dests + (b % dests - j + dests) % dests
            third(source, source).wait_recv()
            third_steps(source, source).wait_recv()
            for k in range(per):
                out[source * per + k] = widen(got[source * per + k], step3_in[source, k:k + 1, :])

        for i in range(steps):
            first(i, 1).wait_send()
            first(i, 0).wait_send()
            second(i).wait_send()
            second_steps(i).wait_send()
        for i in range(1, n_blk):
            peer = (b + i) % n_blk
            third(peer, b).wait_send()
            third_steps(peer, b).wait_send()
            places(peer, b).wait_send()
            places(peer, peer).wait_recv()

    vmem = pl.BlockSpec(memory_space=pltpu.VMEM)
    dma = pltpu.SemaphoreType.DMA
    block = (own_rows, size, size)
    return pl.pallas_call(
        kernel,
        out_shape=(
            jax.ShapeDtypeStruct(block, jnp.float32),
            jax.ShapeDtypeStruct((n_blk, 1, LANES), jnp.int32),
        ),
        in_specs=[pl.BlockSpec(memory_space=pltpu.SMEM)] + [vmem] * 4,
        out_specs=(vmem, vmem),
        scratch_shapes=[
            pltpu.VMEM((hb_rows, size, size), jnp.float32),
            pltpu.VMEM((2,) + block, jnp.float32),
            pltpu.VMEM(block, jnp.int16),
            pltpu.VMEM(block, jnp.int16),
            pltpu.VMEM(block, jnp.int16),
            pltpu.VMEM(block, jnp.int16),
            pltpu.VMEM((steps, 8, size), jnp.float32),
            pltpu.VMEM((steps, 8, size), jnp.float32),
            pltpu.VMEM((n_blk, 8, size), jnp.float32),
            pltpu.VMEM((n_blk, 8, size), jnp.float32),
            dma((2, steps)), dma((2, steps)),
            dma((steps,)), dma((steps,)),
            dma((steps,)), dma((steps,)),
            dma((n_blk,)), dma((n_blk,)),
            dma((n_blk,)), dma((n_blk,)),
            dma((n_blk,)), dma((n_blk,)),
        ],
        compiler_params=pltpu.CompilerParams(
            collective_id=0, has_side_effects=True, vmem_limit_bytes=26 << 20
        ),
    )(keys, integrals, table, extra, pos)


def arrange(blocks, pos, begin):
    n = blocks.shape[0]
    n_blk = pos.shape[0]
    per = n // n_blk

    def kernel(begin_ref, pos_ref, src, dst, sem):
        for s in range(n_blk):
            for k in range(per):
                pltpu.make_async_copy(
                    src.at[s * per + k], dst.at[pos_ref[s, 0, begin_ref[0] + k]], sem
                ).start()
        pltpu.make_async_copy(src, dst, sem).wait()

    smem = pl.BlockSpec(memory_space=pltpu.SMEM)
    return pl.pallas_call(
        kernel,
        out_shape=jax.ShapeDtypeStruct(blocks.shape, jnp.float32),
        in_specs=[smem, smem, pl.BlockSpec(memory_space=pl.ANY)],
        out_specs=pl.BlockSpec(memory_space=pl.ANY),
        scratch_shapes=[pltpu.SemaphoreType.DMA],
        compiler_params=pltpu.CompilerParams(vmem_limit_bytes=2 << 20),
    )(begin, pos, blocks)


def on_device(integrals, densities, entry_block, entry_state, entry_slot, counts, owner):
    hb_rows = owner.shape[0]
    n_tgt = lax.axis_size("tgt")
    n_blk = lax.axis_size("blk")
    own_rows = hb_rows // n_tgt
    t = lax.axis_index("tgt")
    b = lax.axis_index("blk")
    keys, pos, ints, table = route(
        entry_block, entry_state, entry_slot, counts, owner, integrals, densities, own_rows
    )
    extra = spill(keys, ints, table, hb_rows)
    got, where = exchange(keys, ints, table, extra, pos, own_rows, n_blk)
    begin = (t * own_rows + b * (own_rows // n_blk)).reshape(1)
    return arrange(got, where, begin)


def solution(mesh):
    in_specs = (
        P(("tgt", "blk"), None, None),
        P("tgt", None, None),
        P(("tgt", "blk")),
        P(("tgt", "blk")),
        P(("tgt", "blk")),
        P(("tgt", "blk"), None),
        P("blk"),
    )
    out_specs = P(("tgt", "blk"), None, None)
    return jax.shard_map(
        on_device, mesh=mesh, in_specs=in_specs, out_specs=out_specs, check_vma=False
    )
```

```python
import jax
import jax.numpy as jnp
from jax import lax
from jax.experimental import pallas as pl
from jax.experimental.pallas import tpu as pltpu
from jax.sharding import PartitionSpec as P

CAP = 16
CHUNK = 4
UNROLL = 16
STEPS = 8
LAG = 1
PIECES = 5
LANES = 128
MESH = pl.DeviceIdType.MESH
LEVELS = 32767.0
SMALLEST = 1e-33


def route(entry_block, entry_state, entry_slot, counts, owner, integrals, densities, own_rows):
    s_group, size, _ = densities.shape
    states = s_group * lax.axis_size("tgt")
    half = size // 2
    cut = s_group // PIECES
    e_cap = entry_block.shape[0]
    hb_rows = owner.shape[0]
    groups = e_cap // LANES
    flat = (groups, LANES)
    fixed = hb_rows * CAP
    tall = (fixed + e_cap) // LANES

    def kernel(counts_hbm, block_hbm, state_hbm, slot_hbm, owner_hbm, int_hbm, den_hbm,
               keys_ref, pos_ref, ints_ref, table_ref, counts_ref, block_ref, state_ref, slot_ref, owner_ref,
               hot, pre, left, right, sems, y_send, y_recv, x_send, x_recv, c_send, c_recv,
               o_send, o_recv):
        t = lax.axis_index("tgt")
        b = lax.axis_index("blk")
        beside = (t // 2) * 2 + 1 - t % 2
        across = (1 - t // 2) * 2 + t % 2
        beyond = (1 - t // 2) * 2 + 1 - t % 2
        mate = (b // 2) * 2 + 1 - b % 2
        side = b % 2

        def part(group, p, which):
            return table_ref.at[
                pl.ds(1 + group * s_group + p * cut, cut), pl.ds(which * half, half)
            ]

        def over_y(p, to):
            return pltpu.make_async_remote_copy(
                src_ref=den_hbm.at[pl.ds(p * cut, cut), pl.ds(side * half, half)],
                dst_ref=part(to, p, side),
                send_sem=y_send.at[p], recv_sem=y_recv.at[p],
                device_id={"tgt": across}, device_id_type=MESH,
            )

        def over_x(p, which):
            return pltpu.make_async_remote_copy(
                src_ref=part(across, p, which), dst_ref=part(across, p, which),
                send_sem=x_send.at[p], recv_sem=x_recv.at[p],
                device_id={"blk": mate}, device_id_type=MESH,
            )

        def pass_on(group, p, which, i):
            return pltpu.make_async_remote_copy(
                src_ref=part(group, p, which), dst_ref=part(group, p, which),
                send_sem=c_send.at[i, p], recv_sem=c_recv.at[i, p],
                device_id={"tgt": beside}, device_id_type=MESH,
            )

        def share(group):
            return pltpu.make_async_remote_copy(
                src_ref=den_hbm, dst_ref=table_ref.at[pl.ds(1 + group * s_group, s_group)],
                send_sem=o_send, recv_sem=o_recv,
                device_id={"tgt": beside}, device_id_type=MESH,
            )

        barrier = pltpu.get_barrier_semaphore()
        for peer in ({"tgt": beside}, {"tgt": across}, {"blk": mate}):
            pl.semaphore_signal(barrier, inc=1, device_id=peer, device_id_type=MESH)
        moves = (
            (slot_hbm, slot_ref), (owner_hbm, owner_ref), (block_hbm, block_ref),
            (state_hbm, state_ref), (int_hbm, ints_ref),
            (den_hbm, table_ref.at[pl.ds(1 + t * s_group, s_group)]),
            (counts_hbm, counts_ref),
        )
        loads = [
            pltpu.make_async_copy(src, dst, sems.at[i]) for i, (src, dst) in enumerate(moves)
        ]
        for load in loads:
            load.start()
        table_ref[0] = jnp.zeros((size, size), table_ref.dtype)
        pl.semaphore_wait(barrier, 3)
        for p in range(PIECES):
            over_y(p, t).start()
        share(t).start()
        loads[6].wait()
        live = counts_ref[0, 0]
        for i in range(1, counts.shape[1]):
            live = live + counts_ref[0, i]
        lane = lax.broadcasted_iota(jnp.int32, (1, LANES), 1)
        sub = lax.broadcasted_iota(jnp.int32, (hb_rows, LANES), 0)
        wide = lax.broadcasted_iota(jnp.int32, (hb_rows, LANES), 1)
        loads[0].wait()
        for g in range(groups):
            ok = g * LANES + lane < live
            slot = jnp.where(ok, slot_ref[g:g + 1, :], -1)
            hot[g * hb_rows:(g + 1) * hb_rows, :] = jnp.where(
                sub == slot, 1.0, 0.0
            ).astype(jnp.bfloat16)
        before = jnp.where(sub < wide, 1.0, 0.0).astype(jnp.bfloat16)
        after = jnp.where(wide < sub, 1.0, 0.0).astype(jnp.bfloat16)
        ones = jnp.ones((LANES, LANES), jnp.bfloat16)
        counted = jnp.dot(
            hot[...], jnp.concatenate([before, ones], axis=1), preferred_element_type=jnp.float32
        )
        running = jnp.zeros((hb_rows, LANES), jnp.float32)
        for g in range(groups):
            piece = counted[g * hb_rows:(g + 1) * hb_rows]
            pre[g] = piece[:, :LANES] + running
            running = running + piece[:, LANES:]
        for load in loads[1:4]:
            load.wait()
        mine = jnp.broadcast_to(owner_ref[...], (hb_rows, LANES))
        column = jnp.transpose(mine)
        smaller = jnp.where(mine < column, 1.0, 0.0).astype(jnp.bfloat16)
        place = jnp.dot(smaller, ones, preferred_element_type=jnp.float32)
        local = (column % own_rows).astype(jnp.float32)
        pos_ref[0] = jnp.sum(
            jnp.where(place.astype(jnp.int32) == wide, local, 0.0), axis=0, keepdims=True
        ).astype(jnp.int32)
        chunks = jnp.floor((jnp.maximum(running - CAP, 0.0) + (CHUNK - 1)) * (1.0 / CHUNK))
        high = jnp.floor(chunks * (1.0 / 16))
        low = chunks - 16 * high
        start = 16 * jnp.dot(
            after, high.astype(jnp.bfloat16), preferred_element_type=jnp.float32
        ) + jnp.dot(after, low.astype(jnp.bfloat16), preferred_element_type=jnp.float32)
        total = start[hb_rows - 1:, :] + chunks[hb_rows - 1:, :]
        base_fixed = place * CAP
        base_rest = start * CHUNK + (fixed - CAP)
        tall_sub = lax.broadcasted_iota(jnp.int32, (tall, LANES), 0)
        for g in range(groups):
            at = slice(g * LANES, (g + 1) * LANES)
            here = hot[g * hb_rows:(g + 1) * hb_rows, :].astype(jnp.float32)
            seen = pre[g]
            goal = seen + jnp.where(seen < CAP, base_fixed, base_rest)
            goal = jnp.sum(goal * here, axis=0, keepdims=True).astype(jnp.int32)
            row = jnp.sum(place * here, axis=0, keepdims=True)
            ok = g * LANES + lane < live
            goal = jnp.where(ok, goal, -1)
            left[:, at] = jnp.where(tall_sub == goal // LANES, 1.0, 0.0).astype(jnp.bfloat16)
            match = sub == goal % LANES
            digits = (
                block_ref[g:g + 1, :].astype(jnp.float32),
                (state_ref[g:g + 1, :] + 1).astype(jnp.float32),
                row,
            )
            for d, digit in enumerate(digits):
                right[d * LANES:(d + 1) * LANES, at] = jnp.where(match, digit, 0.0).astype(
                    jnp.bfloat16
                )
        table = lax.dot_general(
            left[...], right[...], (((1,), (1,)), ((), ())), preferred_element_type=jnp.float32
        ).astype(jnp.int32)
        keys_ref[:tall] = (
            table[:, :LANES] + (table[:, LANES:2 * LANES] << 8) + (table[:, 2 * LANES:] << 16)
        )
        keys_ref[tall:] = jnp.broadcast_to(total, (8, LANES)).astype(jnp.int32)
        for p in range(PIECES):
            over_y(p, across).wait_recv()
            over_x(p, side).start()
            pass_on(across, p, side, 0).start()
        for p in range(PIECES):
            over_x(p, 1 - side).wait_recv()
            pass_on(across, p, 1 - side, 1).start()
        share(beside).wait_recv()
        for p in range(PIECES):
            pass_on(beyond, p, side, 0).wait_recv()
            pass_on(beyond, p, 1 - side, 1).wait_recv()
        for p in range(PIECES):
            over_y(p, t).wait_send()
            over_x(p, side).wait_send()
            pass_on(across, p, side, 0).wait_send()
            pass_on(across, p, 1 - side, 1).wait_send()
        share(t).wait_send()
        loads[4].wait()
        loads[5].wait()

    vmem = pl.BlockSpec(memory_space=pltpu.VMEM)
    dma = pltpu.SemaphoreType.DMA
    return pl.pallas_call(
        kernel,
        out_shape=(
            jax.ShapeDtypeStruct((tall + 8, LANES), jnp.int32),
            jax.ShapeDtypeStruct((1, 1, LANES), jnp.int32),
            jax.ShapeDtypeStruct(integrals.shape, integrals.dtype),
            jax.ShapeDtypeStruct((states + 1, size, size), densities.dtype),
        ),
        in_specs=[pl.BlockSpec(memory_space=pltpu.HBM)] * 7,
        out_specs=(vmem,) * 4,
        scratch_shapes=[
            pltpu.SMEM(counts.shape, jnp.int32),
            pltpu.VMEM(flat, jnp.int32),
            pltpu.VMEM(flat, jnp.int32),
            pltpu.VMEM(flat, jnp.int32),
            pltpu.VMEM((1, hb_rows), jnp.int32),
            pltpu.VMEM((groups * hb_rows, LANES), jnp.bfloat16),
            pltpu.VMEM((groups, hb_rows, LANES), jnp.float32),
            pltpu.VMEM((tall, e_cap), jnp.bfloat16),
            pltpu.VMEM((3 * LANES, e_cap), jnp.bfloat16),
            dma((7,)),
            dma((PIECES,)), dma((PIECES,)), dma((PIECES,)), dma((PIECES,)),
            dma((2, PIECES)), dma((2, PIECES)), dma, dma,
        ],
        compiler_params=pltpu.CompilerParams(
            collective_id=1, has_side_effects=True, vmem_limit_bytes=38 << 20
        ),
    )(
        *(
            pltpu.with_memory_space_constraint(x, pltpu.HBM)
            for x in (
                counts, entry_block.reshape(flat), entry_state.reshape(flat),
                entry_slot.reshape(flat),
                owner.reshape(1, hb_rows), integrals, densities,
            )
        ),
    )


def spill(keys, integrals, table, hb_rows):
    size = table.shape[-1]
    fixed = hb_rows * CAP
    tall = keys.shape[0] - 8

    def kernel(keys_ref, ints, dens, acc):
        @pl.loop(0, hb_rows)
        def _(j):
            acc[j] = jnp.zeros((size, size), jnp.float32)

        @pl.loop(0, (keys_ref[tall, 0] + UNROLL - 1) // UNROLL)
        def _(step):
            prods = []
            for u in range(UNROLL):
                base = fixed + (step * UNROLL + u) * CHUNK
                ks = [keys_ref[(base + i) >> 7, (base + i) & 127] for i in range(CHUNK)]
                lhs = jnp.concatenate([ints[k & 255] for k in ks], axis=1)
                rhs = jnp.concatenate([dens[(k >> 8) & 255] for k in ks], axis=0)
                prods.append(
                    (ks[0] >> 16, jnp.dot(lhs, rhs, preferred_element_type=jnp.float32))
                )
            for row, prod in prods:
                acc[row] += prod

    vmem = pl.BlockSpec(memory_space=pltpu.VMEM)
    return pl.pallas_call(
        kernel,
        out_shape=jax.ShapeDtypeStruct((hb_rows, size, size), jnp.float32),
        in_specs=[pl.BlockSpec(memory_space=pltpu.SMEM), vmem, vmem],
        out_specs=vmem,
        compiler_params=pltpu.CompilerParams(vmem_limit_bytes=8 << 20),
    )(keys, integrals, table)


def narrow(x):
    top = jnp.maximum(jnp.max(jnp.abs(x), axis=0, keepdims=True), SMALLEST)
    return jnp.round(x * (LEVELS / top)).astype(jnp.int32).astype(jnp.int16), top * (1.0 / LEVELS)


def widen(q, step):
    return q.astype(jnp.int32).astype(jnp.float32) * step


def exchange(keys, integrals, table, extra, pos, own_rows, n_blk):
    size = integrals.shape[-1]
    steps = min(STEPS, n_blk)
    rows = own_rows // steps
    dests = n_blk // steps
    per = own_rows // n_blk
    hb_rows = extra.shape[0]

    def kernel(keys_ref, ints, dens, base, pos_ref, out, pos_out, acc, r1, s2, r2, s3, got,
               step2, step2_in, step3, step3_in, s1_send, s1_recv, s2_send, s2_recv, t2_send,
               t2_recv, s3_send, s3_recv, t3_send, t3_recv, p_send, p_recv):
        t = lax.axis_index("tgt")
        b = lax.axis_index("blk")
        y, c = t // 2, t % 2
        sibling = y * 2 + (1 - c)
        across = (1 - y) * 2 + c
        barrier = pltpu.get_barrier_semaphore()
        pl.semaphore_signal(barrier, inc=1, device_id={"tgt": sibling}, device_id_type=MESH)
        pl.semaphore_signal(barrier, inc=1, device_id={"tgt": across}, device_id_type=MESH)
        for i in range(1, n_blk):
            pl.semaphore_signal(
                barrier, inc=1, device_id={"blk": (b + i) % n_blk}, device_id_type=MESH
            )

        def shift(i):
            return steps // 2 + (1 - 2 * (i % 2)) * ((i + 1) // 2)

        def line(i):
            return (b // dests + shift(i)) % steps

        def span(i):
            return line(i) * rows

        def first(i, far):
            side = 1 - y if far else y
            return pltpu.make_async_remote_copy(
                src_ref=acc.at[pl.ds((side * 2 + 1 - c) * own_rows + span(i), rows)],
                dst_ref=r1.at[far, pl.ds(span(i), rows)],
                send_sem=s1_send.at[far, i],
                recv_sem=s1_recv.at[far, i],
                device_id={"tgt": sibling},
                device_id_type=MESH,
            )

        def second(i):
            return pltpu.make_async_remote_copy(
                src_ref=s2.at[pl.ds(span(i), rows)],
                dst_ref=r2.at[pl.ds(span(i), rows)],
                send_sem=s2_send.at[i],
                recv_sem=s2_recv.at[i],
                device_id={"tgt": across},
                device_id_type=MESH,
            )

        def second_steps(i):
            return pltpu.make_async_remote_copy(
                src_ref=step2.at[i],
                dst_ref=step2_in.at[i],
                send_sem=t2_send.at[i],
                recv_sem=t2_recv.at[i],
                device_id={"tgt": across},
                device_id_type=MESH,
            )

        def third(dest, slot):
            return pltpu.make_async_remote_copy(
                src_ref=s3.at[pl.ds(dest * per, per)],
                dst_ref=got.at[pl.ds(slot * per, per)],
                send_sem=s3_send.at[dest],
                recv_sem=s3_recv.at[slot],
                device_id={"blk": dest},
                device_id_type=MESH,
            )

        def third_steps(dest, slot):
            return pltpu.make_async_remote_copy(
                src_ref=step3.at[dest],
                dst_ref=step3_in.at[slot],
                send_sem=t3_send.at[dest],
                recv_sem=t3_recv.at[slot],
                device_id={"blk": dest},
                device_id_type=MESH,
            )

        def places(dest, slot):
            return pltpu.make_async_remote_copy(
                src_ref=pos_ref.at[0],
                dst_ref=pos_out.at[slot],
                send_sem=p_send.at[dest],
                recv_sem=p_recv.at[slot],
                device_id={"blk": dest},
                device_id_type=MESH,
            )

        def multiply(i, far):
            side = 1 - y if far else y
            for core in (1 - c, c):
                for k in range(rows):
                    row = (side * 2 + core) * own_rows + span(i) + k
                    ks = []
                    for e in range(CAP):
                        at = row * CAP + e
                        ks.append(keys_ref[at // LANES, at % LANES])
                    lhs = jnp.concatenate([ints[key & 255] for key in ks], axis=1)
                    rhs = jnp.concatenate([dens[(key >> 8) & 255] for key in ks], axis=0)
                    acc[row] = base[row] + jnp.dot(lhs, rhs, preferred_element_type=jnp.float32)

        def reduce_far(i):
            for k in range(rows):
                row = span(i) + k
                q, step = narrow(acc[((1 - y) * 2 + c) * own_rows + row] + r1[1, row])
                s2[row] = q
                step2[i, k:k + 1, :] = step
            for k in range(rows, 8):
                step2[i, k:k + 1, :] = jnp.zeros((1, size), jnp.float32)

        def dest_of(i, j):
            return line(i) * dests + (b % dests + j) % dests

        def reduce_near(i, own):
            for j in range(dests):
                dest = dest_of(i, j)
                for k in range(per):
                    row = dest * per + k
                    at = (b % dests + j) % dests * per + k if dests > 1 else k
                    scale = step2_in[i, pl.ds(at, 1), :]
                    total = acc[(y * 2 + c) * own_rows + row] + r1[0, row] + widen(r2[row], scale)
                    if own and j == 0:
                        out[row] = total
                    else:
                        q, step = narrow(total)
                        s3[row] = q
                        step3[dest, k:k + 1, :] = step
                for k in range(per, 8):
                    step3[dest, k:k + 1, :] = jnp.zeros((1, size), jnp.float32)

        def await_near(i):
            first(i, 0).wait_recv()
            second(i).wait_recv()
            second_steps(i).wait_recv()

        def send_far(i):
            second(i).start()
            second_steps(i).start()

        def send_near(i, own):
            for j in range(1 if own else 0, dests):
                dest = dest_of(i, j)
                third(dest, b).start()
                third_steps(dest, b).start()

        multiply(0, 1)
        pl.semaphore_wait(barrier, n_blk + 1)
        first(0, 1).start()
        for i in range(1, n_blk):
            places((b + i) % n_blk, b).start()
        pos_out[b] = pos_ref[0]

        def finish(i, own):
            await_near(i)
            reduce_near(i, own)
            send_near(i, own)

        def turn(i, carry):
            @pl.when(i + 1 < steps)
            def _():
                multiply(i + 1, 1)
                first(i + 1, 1).start()

            first(i, 1).wait_recv()
            reduce_far(i)
            send_far(i)
            multiply(i, 0)
            first(i, 0).start()

            @pl.when(i >= LAG)
            def _():
                finish(i - LAG, False)

            return carry

        lax.fori_loop(0, steps, turn, 0)
        for i in range(steps - LAG, steps):
            finish(i, i == steps - 1)

        def arrive(i, carry):
            for j in range(dests):
                source = (b // dests - shift(i) + steps) % steps * dests
                source = source + (b % dests - j + dests) % dests
                third(source, source).wait_recv()
                third_steps(source, source).wait_recv()
                for k in range(per):
                    out[source * per + k] = widen(
                        got[source * per + k], step3_in[source, k:k + 1, :]
                    )
            return carry

        lax.fori_loop(0, steps - 1, arrive, 0)
        for j in range(1, dests):
            source = b // dests * dests + (b % dests - j + dests) % dests
            third(source, source).wait_recv()
            third_steps(source, source).wait_recv()
            for k in range(per):
                out[source * per + k] = widen(got[source * per + k], step3_in[source, k:k + 1, :])

        for i in range(steps):
            first(i, 1).wait_send()
            first(i, 0).wait_send()
            second(i).wait_send()
            second_steps(i).wait_send()
        for i in range(1, n_blk):
            peer = (b + i) % n_blk
            third(peer, b).wait_send()
            third_steps(peer, b).wait_send()
            places(peer, b).wait_send()
            places(peer, peer).wait_recv()

    vmem = pl.BlockSpec(memory_space=pltpu.VMEM)
    dma = pltpu.SemaphoreType.DMA
    block = (own_rows, size, size)
    return pl.pallas_call(
        kernel,
        out_shape=(
            jax.ShapeDtypeStruct(block, jnp.float32),
            jax.ShapeDtypeStruct((n_blk, 1, LANES), jnp.int32),
        ),
        in_specs=[pl.BlockSpec(memory_space=pltpu.SMEM)] + [vmem] * 4,
        out_specs=(vmem, vmem),
        scratch_shapes=[
            pltpu.VMEM((hb_rows, size, size), jnp.float32),
            pltpu.VMEM((2,) + block, jnp.float32),
            pltpu.VMEM(block, jnp.int16),
            pltpu.VMEM(block, jnp.int16),
            pltpu.VMEM(block, jnp.int16),
            pltpu.VMEM(block, jnp.int16),
            pltpu.VMEM((steps, 8, size), jnp.float32),
            pltpu.VMEM((steps, 8, size), jnp.float32),
            pltpu.VMEM((n_blk, 8, size), jnp.float32),
            pltpu.VMEM((n_blk, 8, size), jnp.float32),
            dma((2, steps)), dma((2, steps)),
            dma((steps,)), dma((steps,)),
            dma((steps,)), dma((steps,)),
            dma((n_blk,)), dma((n_blk,)),
            dma((n_blk,)), dma((n_blk,)),
            dma((n_blk,)), dma((n_blk,)),
        ],
        compiler_params=pltpu.CompilerParams(
            collective_id=0, has_side_effects=True, vmem_limit_bytes=26 << 20
        ),
    )(keys, integrals, table, extra, pos)


def arrange(blocks, pos, begin):
    n = blocks.shape[0]
    n_blk = pos.shape[0]
    per = n // n_blk

    def kernel(begin_ref, pos_ref, src, dst, sem):
        for s in range(n_blk):
            for k in range(per):
                pltpu.make_async_copy(
                    src.at[s * per + k], dst.at[pos_ref[s, 0, begin_ref[0] + k]], sem
                ).start()
        pltpu.make_async_copy(src, dst, sem).wait()

    smem = pl.BlockSpec(memory_space=pltpu.SMEM)
    return pl.pallas_call(
        kernel,
        out_shape=jax.ShapeDtypeStruct(blocks.shape, jnp.float32),
        in_specs=[smem, smem, pl.BlockSpec(memory_space=pl.ANY)],
        out_specs=pl.BlockSpec(memory_space=pl.ANY),
        scratch_shapes=[pltpu.SemaphoreType.DMA],
        compiler_params=pltpu.CompilerParams(vmem_limit_bytes=2 << 20),
    )(begin, pos, blocks)


def on_device(integrals, densities, entry_block, entry_state, entry_slot, counts, owner):
    hb_rows = owner.shape[0]
    n_tgt = lax.axis_size("tgt")
    n_blk = lax.axis_size("blk")
    own_rows = hb_rows // n_tgt
    t = lax.axis_index("tgt")
    b = lax.axis_index("blk")
    keys, pos, ints, table = route(
        entry_block, entry_state, entry_slot, counts, owner, integrals, densities, own_rows
    )
    extra = spill(keys, ints, table, hb_rows)
    got, where = exchange(keys, ints, table, extra, pos, own_rows, n_blk)
    begin = (t * own_rows + b * (own_rows // n_blk)).reshape(1)
    return arrange(got, where, begin)


def solution(mesh):
    in_specs = (
        P(("tgt", "blk"), None, None),
        P("tgt", None, None),
        P(("tgt", "blk")),
        P(("tgt", "blk")),
        P(("tgt", "blk")),
        P(("tgt", "blk"), None),
        P("blk"),
    )
    out_specs = P(("tgt", "blk"), None, None)
    return jax.shard_map(
        on_device, mesh=mesh, in_specs=in_specs, out_specs=out_specs, check_vma=False
    )
```

```python
import jax
import jax.numpy as jnp
from jax import lax
from jax.experimental import pallas as pl
from jax.experimental.pallas import tpu as pltpu
from jax.sharding import PartitionSpec as P

CAP = 16
CHUNK = 4
UNROLL = 16
STEPS = 8
LAG = 1
PIECES = 3
LANES = 128
MESH = pl.DeviceIdType.MESH
LEVELS = 32767.0
SMALLEST = 1e-33


def route(entry_block, entry_state, entry_slot, counts, owner, integrals, densities, own_rows):
    s_group, size, _ = densities.shape
    states = s_group * lax.axis_size("tgt")
    quarter = size // 4
    cut = s_group // PIECES
    e_cap = entry_block.shape[0]
    hb_rows = owner.shape[0]
    groups = e_cap // LANES
    flat = (groups, LANES)
    fixed = hb_rows * CAP
    tall = (fixed + e_cap) // LANES

    def kernel(counts_hbm, block_hbm, state_hbm, slot_hbm, owner_hbm, int_hbm, den_hbm,
               keys_ref, pos_ref, ints_ref, table_ref, base_ref, counts_ref, block_ref, state_ref, slot_ref, owner_ref,
               hot, pre, left, right, sems, y_send, y_recv, x_send, x_recv, c_send, c_recv,
               o_send, o_recv):
        t = lax.axis_index("tgt")
        b = lax.axis_index("blk")
        beside = (t // 2) * 2 + 1 - t % 2
        across = (1 - t // 2) * 2 + t % 2
        beyond = (1 - t // 2) * 2 + 1 - t % 2
        x, z = b % 2, b // 2 % 2
        mates = (b + 1 - 2 * x, b + 2 - 4 * z)
        mine = 2 * z + x
        theirs = (2 * z + 1 - x, 2 * (1 - z) + x)
        rest = 3 - mine

        def part(group, p, which):
            return table_ref.at[
                pl.ds(1 + group * s_group + p * cut, cut), pl.ds(which * quarter, quarter)
            ]

        def over_y(p, to, i):
            which = rest if i else mine
            return pltpu.make_async_remote_copy(
                src_ref=den_hbm.at[pl.ds(p * cut, cut), pl.ds(which * quarter, quarter)],
                dst_ref=part(to, p, which),
                send_sem=y_send.at[i, p], recv_sem=y_recv.at[i, p],
                device_id={"tgt": across}, device_id_type=MESH,
            )

        def relay(p, which, i):
            return pltpu.make_async_remote_copy(
                src_ref=part(across, p, which), dst_ref=part(across, p, which),
                send_sem=x_send.at[i, p], recv_sem=x_recv.at[i, p],
                device_id={"blk": mates[i]}, device_id_type=MESH,
            )

        def pass_on(group, p, which):
            return pltpu.make_async_remote_copy(
                src_ref=part(group, p, which), dst_ref=part(group, p, which),
                send_sem=c_send.at[which, p], recv_sem=c_recv.at[which, p],
                device_id={"tgt": beside}, device_id_type=MESH,
            )

        def share(group):
            return pltpu.make_async_remote_copy(
                src_ref=den_hbm, dst_ref=table_ref.at[pl.ds(1 + group * s_group, s_group)],
                send_sem=o_send, recv_sem=o_recv,
                device_id={"tgt": beside}, device_id_type=MESH,
            )

        barrier = pltpu.get_barrier_semaphore()
        for peer in ({"tgt": beside}, {"tgt": across}, {"blk": mates[0]}, {"blk": mates[1]}):
            pl.semaphore_signal(barrier, inc=1, device_id=peer, device_id_type=MESH)
        moves = (
            (slot_hbm, slot_ref), (owner_hbm, owner_ref), (block_hbm, block_ref),
            (state_hbm, state_ref), (int_hbm, ints_ref),
            (den_hbm, table_ref.at[pl.ds(1 + t * s_group, s_group)]),
            (counts_hbm, counts_ref),
        )
        loads = [
            pltpu.make_async_copy(src, dst, sems.at[i]) for i, (src, dst) in enumerate(moves)
        ]
        for load in loads:
            load.start()
        table_ref[0] = jnp.zeros((size, size), table_ref.dtype)
        pl.semaphore_wait(barrier, 4)
        for i in range(2):
            for p in range(PIECES):
                over_y(p, t, i).start()
        share(t).start()
        loads[6].wait()
        live = counts_ref[0, 0]
        for i in range(1, counts.shape[1]):
            live = live + counts_ref[0, i]
        lane = lax.broadcasted_iota(jnp.int32, (1, LANES), 1)
        sub = lax.broadcasted_iota(jnp.int32, (hb_rows, LANES), 0)
        wide = lax.broadcasted_iota(jnp.int32, (hb_rows, LANES), 1)
        loads[0].wait()
        for g in range(groups):
            ok = g * LANES + lane < live
            slot = jnp.where(ok, slot_ref[g:g + 1, :], -1)
            hot[g * hb_rows:(g + 1) * hb_rows, :] = jnp.where(
                sub == slot, 1.0, 0.0
            ).astype(jnp.bfloat16)
        before = jnp.where(sub < wide, 1.0, 0.0).astype(jnp.bfloat16)
        after = jnp.where(wide < sub, 1.0, 0.0).astype(jnp.bfloat16)
        ones = jnp.ones((LANES, LANES), jnp.bfloat16)
        counted = jnp.dot(
            hot[...], jnp.concatenate([before, ones], axis=1), preferred_element_type=jnp.float32
        )
        running = jnp.zeros((hb_rows, LANES), jnp.float32)
        for g in range(groups):
            piece = counted[g * hb_rows:(g + 1) * hb_rows]
            pre[g] = piece[:, :LANES] + running
            running = running + piece[:, LANES:]
        for load in loads[1:4]:
            load.wait()
        every = jnp.broadcast_to(owner_ref[...], (hb_rows, LANES))
        column = jnp.transpose(every)
        smaller = jnp.where(every < column, 1.0, 0.0).astype(jnp.bfloat16)
        place = jnp.dot(smaller, ones, preferred_element_type=jnp.float32)
        local = (column % own_rows).astype(jnp.float32)
        pos_ref[0] = jnp.sum(
            jnp.where(place.astype(jnp.int32) == wide, local, 0.0), axis=0, keepdims=True
        ).astype(jnp.int32)
        chunks = jnp.floor((jnp.maximum(running - CAP, 0.0) + (CHUNK - 1)) * (1.0 / CHUNK))
        high = jnp.floor(chunks * (1.0 / 16))
        low = chunks - 16 * high
        start = 16 * jnp.dot(
            after, high.astype(jnp.bfloat16), preferred_element_type=jnp.float32
        ) + jnp.dot(after, low.astype(jnp.bfloat16), preferred_element_type=jnp.float32)
        total = start[hb_rows - 1:, :] + chunks[hb_rows - 1:, :]
        base_fixed = place * CAP
        base_rest = start * CHUNK + (fixed - CAP)
        tall_sub = lax.broadcasted_iota(jnp.int32, (tall, LANES), 0)
        for g in range(groups):
            at = slice(g * LANES, (g + 1) * LANES)
            here = hot[g * hb_rows:(g + 1) * hb_rows, :].astype(jnp.float32)
            seen = pre[g]
            goal = seen + jnp.where(seen < CAP, base_fixed, base_rest)
            goal = jnp.sum(goal * here, axis=0, keepdims=True).astype(jnp.int32)
            row = jnp.sum(place * here, axis=0, keepdims=True)
            ok = g * LANES + lane < live
            goal = jnp.where(ok, goal, -1)
            left[:, at] = jnp.where(tall_sub == goal // LANES, 1.0, 0.0).astype(jnp.bfloat16)
            match = sub == goal % LANES
            digits = (
                block_ref[g:g + 1, :].astype(jnp.float32),
                (state_ref[g:g + 1, :] + 1).astype(jnp.float32),
                row,
            )
            for d, digit in enumerate(digits):
                right[d * LANES:(d + 1) * LANES, at] = jnp.where(match, digit, 0.0).astype(
                    jnp.bfloat16
                )
        table = lax.dot_general(
            left[...], right[...], (((1,), (1,)), ((), ())), preferred_element_type=jnp.float32
        ).astype(jnp.int32)
        keys_ref[:tall] = (
            table[:, :LANES] + (table[:, LANES:2 * LANES] << 8) + (table[:, 2 * LANES:] << 16)
        )
        keys_ref[tall:] = jnp.broadcast_to(total, (8, LANES)).astype(jnp.int32)
        @pl.loop(0, hb_rows)
        def _(j):
            base_ref[j] = jnp.zeros((size, size), jnp.float32)

        for p in range(PIECES):
            over_y(p, across, 0).wait_recv()
            for i in range(2):
                relay(p, mine, i).start()
            pass_on(across, p, mine).start()
        for p in range(PIECES):
            for i in range(2):
                relay(p, theirs[i], i).wait_recv()
                pass_on(across, p, theirs[i]).start()
            over_y(p, across, 1).wait_recv()
            pass_on(across, p, rest).start()
        share(beside).wait_recv()
        for p in range(PIECES):
            for which in range(4):
                pass_on(beyond, p, which).wait_recv()
        for p in range(PIECES):
            for i in range(2):
                over_y(p, t, i).wait_send()
                relay(p, mine, i).wait_send()
            for which in range(4):
                pass_on(across, p, which).wait_send()
        share(t).wait_send()
        loads[4].wait()
        loads[5].wait()

    vmem = pl.BlockSpec(memory_space=pltpu.VMEM)
    dma = pltpu.SemaphoreType.DMA
    return pl.pallas_call(
        kernel,
        out_shape=(
            jax.ShapeDtypeStruct((tall + 8, LANES), jnp.int32),
            jax.ShapeDtypeStruct((1, 1, LANES), jnp.int32),
            jax.ShapeDtypeStruct(integrals.shape, integrals.dtype),
            jax.ShapeDtypeStruct((states + 1, size, size), densities.dtype),
            jax.ShapeDtypeStruct((hb_rows, size, size), jnp.float32),
        ),
        in_specs=[pl.BlockSpec(memory_space=pltpu.HBM)] * 7,
        out_specs=(vmem,) * 5,
        scratch_shapes=[
            pltpu.SMEM(counts.shape, jnp.int32),
            pltpu.VMEM(flat, jnp.int32),
            pltpu.VMEM(flat, jnp.int32),
            pltpu.VMEM(flat, jnp.int32),
            pltpu.VMEM((1, hb_rows), jnp.int32),
            pltpu.VMEM((groups * hb_rows, LANES), jnp.bfloat16),
            pltpu.VMEM((groups, hb_rows, LANES), jnp.float32),
            pltpu.VMEM((tall, e_cap), jnp.bfloat16),
            pltpu.VMEM((3 * LANES, e_cap), jnp.bfloat16),
            dma((7,)),
            dma((2, PIECES)), dma((2, PIECES)), dma((2, PIECES)), dma((2, PIECES)),
            dma((4, PIECES)), dma((4, PIECES)), dma, dma,
        ],
        compiler_params=pltpu.CompilerParams(
            collective_id=1, has_side_effects=True, vmem_limit_bytes=34 << 20
        ),
    )(
        *(
            pltpu.with_memory_space_constraint(x, pltpu.HBM)
            for x in (
                counts, entry_block.reshape(flat), entry_state.reshape(flat),
                entry_slot.reshape(flat),
                owner.reshape(1, hb_rows), integrals, densities,
            )
        ),
    )


def spill(keys, integrals, table, zeros):
    hb_rows, size, _ = zeros.shape
    fixed = hb_rows * CAP
    tall = keys.shape[0] - 8

    def kernel(keys_ref, ints, dens, zeros_ref, acc):
        del zeros_ref

        @pl.loop(0, (keys_ref[tall, 0] + UNROLL - 1) // UNROLL)
        def _(step):
            prods = []
            for u in range(UNROLL):
                base = fixed + (step * UNROLL + u) * CHUNK
                ks = [keys_ref[(base + i) >> 7, (base + i) & 127] for i in range(CHUNK)]
                lhs = jnp.concatenate([ints[k & 255] for k in ks], axis=1)
                rhs = jnp.concatenate([dens[(k >> 8) & 255] for k in ks], axis=0)
                prods.append(
                    (ks[0] >> 16, jnp.dot(lhs, rhs, preferred_element_type=jnp.float32))
                )
            for row, prod in prods:
                acc[row] += prod

    vmem = pl.BlockSpec(memory_space=pltpu.VMEM)
    return pl.pallas_call(
        kernel,
        out_shape=jax.ShapeDtypeStruct((hb_rows, size, size), jnp.float32),
        in_specs=[pl.BlockSpec(memory_space=pltpu.SMEM), vmem, vmem, vmem],
        out_specs=vmem,
        input_output_aliases={3: 0},
        compiler_params=pltpu.CompilerParams(vmem_limit_bytes=8 << 20),
    )(keys, integrals, table, zeros)


def narrow(x):
    top = jnp.maximum(jnp.max(jnp.abs(x), axis=0, keepdims=True), SMALLEST)
    return jnp.round(x * (LEVELS / top)).astype(jnp.int32).astype(jnp.int16), top * (1.0 / LEVELS)


def widen(q, step):
    return q.astype(jnp.int32).astype(jnp.float32) * step


def exchange(keys, integrals, table, extra, pos, own_rows, n_blk):
    size = integrals.shape[-1]
    steps = min(STEPS, n_blk)
    rows = own_rows // steps
    dests = n_blk // steps
    per = own_rows // n_blk
    hb_rows = extra.shape[0]

    def kernel(keys_ref, ints, dens, base, pos_ref, out, pos_out, acc, r1, s2, r2, s3, got,
               step2, step2_in, step3, step3_in, s1_send, s1_recv, s2_send, s2_recv, t2_send,
               t2_recv, s3_send, s3_recv, t3_send, t3_recv, p_send, p_recv):
        t = lax.axis_index("tgt")
        b = lax.axis_index("blk")
        y, c = t // 2, t % 2
        sibling = y * 2 + (1 - c)
        across = (1 - y) * 2 + c
        barrier = pltpu.get_barrier_semaphore()
        pl.semaphore_signal(barrier, inc=1, device_id={"tgt": sibling}, device_id_type=MESH)
        pl.semaphore_signal(barrier, inc=1, device_id={"tgt": across}, device_id_type=MESH)
        for i in range(1, n_blk):
            pl.semaphore_signal(
                barrier, inc=1, device_id={"blk": (b + i) % n_blk}, device_id_type=MESH
            )

        def shift(i):
            return steps // 2 + (1 - 2 * (i % 2)) * ((i + 1) // 2)

        def line(i):
            return (b // dests + shift(i)) % steps

        def span(i):
            return line(i) * rows

        def first(i, far):
            side = 1 - y if far else y
            return pltpu.make_async_remote_copy(
                src_ref=acc.at[pl.ds((side * 2 + 1 - c) * own_rows + span(i), rows)],
                dst_ref=r1.at[far, pl.ds(span(i), rows)],
                send_sem=s1_send.at[far, i],
                recv_sem=s1_recv.at[far, i],
                device_id={"tgt": sibling},
                device_id_type=MESH,
            )

        def second(i):
            return pltpu.make_async_remote_copy(
                src_ref=s2.at[pl.ds(span(i), rows)],
                dst_ref=r2.at[pl.ds(span(i), rows)],
                send_sem=s2_send.at[i],
                recv_sem=s2_recv.at[i],
                device_id={"tgt": across},
                device_id_type=MESH,
            )

        def second_steps(i):
            return pltpu.make_async_remote_copy(
                src_ref=step2.at[i],
                dst_ref=step2_in.at[i],
                send_sem=t2_send.at[i],
                recv_sem=t2_recv.at[i],
                device_id={"tgt": across},
                device_id_type=MESH,
            )

        def third(dest, slot):
            return pltpu.make_async_remote_copy(
                src_ref=s3.at[pl.ds(dest * per, per)],
                dst_ref=got.at[pl.ds(slot * per, per)],
                send_sem=s3_send.at[dest],
                recv_sem=s3_recv.at[slot],
                device_id={"blk": dest},
                device_id_type=MESH,
            )

        def third_steps(dest, slot):
            return pltpu.make_async_remote_copy(
                src_ref=step3.at[dest],
                dst_ref=step3_in.at[slot],
                send_sem=t3_send.at[dest],
                recv_sem=t3_recv.at[slot],
                device_id={"blk": dest},
                device_id_type=MESH,
            )

        def places(dest, slot):
            return pltpu.make_async_remote_copy(
                src_ref=pos_ref.at[0],
                dst_ref=pos_out.at[slot],
                send_sem=p_send.at[dest],
                recv_sem=p_recv.at[slot],
                device_id={"blk": dest},
                device_id_type=MESH,
            )

        def multiply(i, far):
            side = 1 - y if far else y
            for core in (1 - c, c):
                for k in range(rows):
                    row = (side * 2 + core) * own_rows + span(i) + k
                    ks = []
                    for e in range(CAP):
                        at = row * CAP + e
                        ks.append(keys_ref[at // LANES, at % LANES])
                    lhs = jnp.concatenate([ints[key & 255] for key in ks], axis=1)
                    rhs = jnp.concatenate([dens[(key >> 8) & 255] for key in ks], axis=0)
                    acc[row] = base[row] + jnp.dot(lhs, rhs, preferred_element_type=jnp.float32)

        def reduce_far(i):
            for k in range(rows):
                row = span(i) + k
                q, step = narrow(acc[((1 - y) * 2 + c) * own_rows + row] + r1[1, row])
                s2[row] = q
                step2[i, k:k + 1, :] = step
            for k in range(rows, 8):
                step2[i, k:k + 1, :] = jnp.zeros((1, size), jnp.float32)

        def dest_of(i, j):
            return line(i) * dests + (b % dests + j) % dests

        def reduce_near(i, own):
            for j in range(dests):
                dest = dest_of(i, j)
                for k in range(per):
                    row = dest * per + k
                    at = (b % dests + j) % dests * per + k if dests > 1 else k
                    scale = step2_in[i, pl.ds(at, 1), :]
                    total = acc[(y * 2 + c) * own_rows + row] + r1[0, row] + widen(r2[row], scale)
                    if own and j == 0:
                        out[row] = total
                    else:
                        q, step = narrow(total)
                        s3[row] = q
                        step3[dest, k:k + 1, :] = step
                for k in range(per, 8):
                    step3[dest, k:k + 1, :] = jnp.zeros((1, size), jnp.float32)

        def await_near(i):
            first(i, 0).wait_recv()
            second(i).wait_recv()
            second_steps(i).wait_recv()

        def send_far(i):
            second(i).start()
            second_steps(i).start()

        def send_near(i, own):
            for j in range(1 if own else 0, dests):
                dest = dest_of(i, j)
                third(dest, b).start()
                third_steps(dest, b).start()

        multiply(0, 1)
        pl.semaphore_wait(barrier, n_blk + 1)
        first(0, 1).start()
        for i in range(1, n_blk):
            places((b + i) % n_blk, b).start()
        pos_out[b] = pos_ref[0]

        def finish(i, own):
            await_near(i)
            reduce_near(i, own)
            send_near(i, own)

        def turn(i, carry):
            @pl.when(i + 1 < steps)
            def _():
                multiply(i + 1, 1)
                first(i + 1, 1).start()

            first(i, 1).wait_recv()
            reduce_far(i)
            send_far(i)
            multiply(i, 0)
            first(i, 0).start()

            @pl.when(i >= LAG)
            def _():
                finish(i - LAG, False)

            return carry

        lax.fori_loop(0, steps, turn, 0)
        for i in range(steps - LAG, steps):
            finish(i, i == steps - 1)

        def arrive(i, carry):
            for j in range(dests):
                source = (b // dests - shift(i) + steps) % steps * dests
                source = source + (b % dests - j + dests) % dests
                third(source, source).wait_recv()
                third_steps(source, source).wait_recv()
                for k in range(per):
                    out[source * per + k] = widen(
                        got[source * per + k], step3_in[source, k:k + 1, :]
                    )
            return carry

        lax.fori_loop(0, steps - 1, arrive, 0)
        for j in range(1, dests):
            source = b // dests * dests + (b % dests - j + dests) % dests
            third(source, source).wait_recv()
            third_steps(source, source).wait_recv()
            for k in range(per):
                out[source * per + k] = widen(got[source * per + k], step3_in[source, k:k + 1, :])

        for i in range(steps):
            first(i, 1).wait_send()
            first(i, 0).wait_send()
            second(i).wait_send()
            second_steps(i).wait_send()
        for i in range(1, n_blk):
            peer = (b + i) % n_blk
            third(peer, b).wait_send()
            third_steps(peer, b).wait_send()
            places(peer, b).wait_send()
            places(peer, peer).wait_recv()

    vmem = pl.BlockSpec(memory_space=pltpu.VMEM)
    dma = pltpu.SemaphoreType.DMA
    block = (own_rows, size, size)
    return pl.pallas_call(
        kernel,
        out_shape=(
            jax.ShapeDtypeStruct(block, jnp.float32),
            jax.ShapeDtypeStruct((n_blk, 1, LANES), jnp.int32),
        ),
        in_specs=[pl.BlockSpec(memory_space=pltpu.SMEM)] + [vmem] * 4,
        out_specs=(vmem, vmem),
        scratch_shapes=[
            pltpu.VMEM((hb_rows, size, size), jnp.float32),
            pltpu.VMEM((2,) + block, jnp.float32),
            pltpu.VMEM(block, jnp.int16),
            pltpu.VMEM(block, jnp.int16),
            pltpu.VMEM(block, jnp.int16),
            pltpu.VMEM(block, jnp.int16),
            pltpu.VMEM((steps, 8, size), jnp.float32),
            pltpu.VMEM((steps, 8, size), jnp.float32),
            pltpu.VMEM((n_blk, 8, size), jnp.float32),
            pltpu.VMEM((n_blk, 8, size), jnp.float32),
            dma((2, steps)), dma((2, steps)),
            dma((steps,)), dma((steps,)),
            dma((steps,)), dma((steps,)),
            dma((n_blk,)), dma((n_blk,)),
            dma((n_blk,)), dma((n_blk,)),
            dma((n_blk,)), dma((n_blk,)),
        ],
        compiler_params=pltpu.CompilerParams(
            collective_id=0, has_side_effects=True, vmem_limit_bytes=22 << 20
        ),
    )(keys, integrals, table, extra, pos)


def arrange(blocks, pos, begin):
    n = blocks.shape[0]
    n_blk = pos.shape[0]
    per = n // n_blk

    def kernel(begin_ref, pos_ref, src, dst, sem):
        for s in range(n_blk):
            for k in range(per):
                pltpu.make_async_copy(
                    src.at[s * per + k], dst.at[pos_ref[s, 0, begin_ref[0] + k]], sem
                ).start()
        pltpu.make_async_copy(src, dst, sem).wait()

    smem = pl.BlockSpec(memory_space=pltpu.SMEM)
    return pl.pallas_call(
        kernel,
        out_shape=jax.ShapeDtypeStruct(blocks.shape, jnp.float32),
        in_specs=[smem, smem, pl.BlockSpec(memory_space=pl.ANY)],
        out_specs=pl.BlockSpec(memory_space=pl.ANY),
        scratch_shapes=[pltpu.SemaphoreType.DMA],
        compiler_params=pltpu.CompilerParams(vmem_limit_bytes=2 << 20),
    )(begin, pos, blocks)


def on_device(integrals, densities, entry_block, entry_state, entry_slot, counts, owner):
    hb_rows = owner.shape[0]
    n_tgt = lax.axis_size("tgt")
    n_blk = lax.axis_size("blk")
    own_rows = hb_rows // n_tgt
    t = lax.axis_index("tgt")
    b = lax.axis_index("blk")
    keys, pos, ints, table, zeros = route(
        entry_block, entry_state, entry_slot, counts, owner, integrals, densities, own_rows
    )
    extra = spill(keys, ints, table, zeros)
    got, where = exchange(keys, ints, table, extra, pos, own_rows, n_blk)
    begin = (t * own_rows + b * (own_rows // n_blk)).reshape(1)
    return arrange(got, where, begin)


def solution(mesh):
    in_specs = (
        P(("tgt", "blk"), None, None),
        P("tgt", None, None),
        P(("tgt", "blk")),
        P(("tgt", "blk")),
        P(("tgt", "blk")),
        P(("tgt", "blk"), None),
        P("blk"),
    )
    out_specs = P(("tgt", "blk"), None, None)
    return jax.shard_map(
        on_device, mesh=mesh, in_specs=in_specs, out_specs=out_specs, check_vma=False
    )
```

```python
import jax
import jax.numpy as jnp
from jax import lax
from jax.experimental import pallas as pl
from jax.experimental.pallas import tpu as pltpu
from jax.sharding import PartitionSpec as P

CAP = 16
CHUNK = 4
UNROLL = 16
STEPS = 8
LAG = 1
PIECES = 3
LANES = 128
MESH = pl.DeviceIdType.MESH
LEVELS = 32767.0
SMALLEST = 1e-33


def route(entry_block, entry_state, entry_slot, counts, owner, integrals, densities, own_rows):
    s_group, size, _ = densities.shape
    states = s_group * lax.axis_size("tgt")
    quarter = size // 4
    cut = s_group // PIECES
    e_cap = entry_block.shape[0]
    hb_rows = owner.shape[0]
    groups = e_cap // LANES
    flat = (groups, LANES)
    fixed = hb_rows * CAP
    tall = (fixed + e_cap) // LANES

    def kernel(counts_hbm, block_hbm, state_hbm, slot_hbm, owner_hbm, int_hbm, den_hbm,
               keys_ref, more_ref, pos_ref, ints_ref, table_ref, base_ref, counts_ref, block_ref, state_ref, slot_ref, owner_ref,
               hot, pre, left, right, sems, y_send, y_recv, x_send, x_recv, c_send, c_recv,
               o_send, o_recv):
        t = lax.axis_index("tgt")
        b = lax.axis_index("blk")
        beside = (t // 2) * 2 + 1 - t % 2
        across = (1 - t // 2) * 2 + t % 2
        beyond = (1 - t // 2) * 2 + 1 - t % 2
        x, z = b % 2, b // 2 % 2
        mates = (b + 1 - 2 * x, b + 2 - 4 * z)
        mine = 2 * z + x
        theirs = (2 * z + 1 - x, 2 * (1 - z) + x)
        rest = 3 - mine

        def part(group, p, which):
            return table_ref.at[
                pl.ds(1 + group * s_group + p * cut, cut), pl.ds(which * quarter, quarter)
            ]

        def over_y(p, to, i):
            which = rest if i else mine
            return pltpu.make_async_remote_copy(
                src_ref=den_hbm.at[pl.ds(p * cut, cut), pl.ds(which * quarter, quarter)],
                dst_ref=part(to, p, which),
                send_sem=y_send.at[i, p], recv_sem=y_recv.at[i, p],
                device_id={"tgt": across}, device_id_type=MESH,
            )

        def relay(p, which, i):
            return pltpu.make_async_remote_copy(
                src_ref=part(across, p, which), dst_ref=part(across, p, which),
                send_sem=x_send.at[i, p], recv_sem=x_recv.at[i, p],
                device_id={"blk": mates[i]}, device_id_type=MESH,
            )

        def pass_on(group, p, which):
            return pltpu.make_async_remote_copy(
                src_ref=part(group, p, which), dst_ref=part(group, p, which),
                send_sem=c_send.at[which, p], recv_sem=c_recv.at[which, p],
                device_id={"tgt": beside}, device_id_type=MESH,
            )

        def share(group):
            return pltpu.make_async_remote_copy(
                src_ref=den_hbm, dst_ref=table_ref.at[pl.ds(1 + group * s_group, s_group)],
                send_sem=o_send, recv_sem=o_recv,
                device_id={"tgt": beside}, device_id_type=MESH,
            )

        def spread(p):
            over_y(p, across, 0).wait_recv()
            for i in range(2):
                relay(p, mine, i).start()
            pass_on(across, p, mine).start()

        barrier = pltpu.get_barrier_semaphore()
        for peer in ({"tgt": beside}, {"tgt": across}, {"blk": mates[0]}, {"blk": mates[1]}):
            pl.semaphore_signal(barrier, inc=1, device_id=peer, device_id_type=MESH)
        moves = (
            (slot_hbm, slot_ref), (owner_hbm, owner_ref), (block_hbm, block_ref),
            (state_hbm, state_ref), (int_hbm, ints_ref),
            (den_hbm, table_ref.at[pl.ds(1 + t * s_group, s_group)]),
            (counts_hbm, counts_ref),
        )
        loads = [
            pltpu.make_async_copy(src, dst, sems.at[i]) for i, (src, dst) in enumerate(moves)
        ]
        for load in loads:
            load.start()
        table_ref[0] = jnp.zeros((size, size), table_ref.dtype)
        pl.semaphore_wait(barrier, 4)
        for i in range(2):
            for p in range(PIECES):
                over_y(p, t, i).start()
        share(t).start()
        loads[6].wait()
        live = counts_ref[0, 0]
        for i in range(1, counts.shape[1]):
            live = live + counts_ref[0, i]
        lane = lax.broadcasted_iota(jnp.int32, (1, LANES), 1)
        sub = lax.broadcasted_iota(jnp.int32, (hb_rows, LANES), 0)
        wide = lax.broadcasted_iota(jnp.int32, (hb_rows, LANES), 1)
        loads[0].wait()
        for g in range(groups):
            ok = g * LANES + lane < live
            slot = jnp.where(ok, slot_ref[g:g + 1, :], -1)
            hot[g * hb_rows:(g + 1) * hb_rows, :] = jnp.where(
                sub == slot, 1.0, 0.0
            ).astype(jnp.bfloat16)
        before = jnp.where(sub < wide, 1.0, 0.0).astype(jnp.bfloat16)
        after = jnp.where(wide < sub, 1.0, 0.0).astype(jnp.bfloat16)
        ones = jnp.ones((LANES, LANES), jnp.bfloat16)
        counted = jnp.dot(
            hot[...], jnp.concatenate([before, ones], axis=1), preferred_element_type=jnp.float32
        )
        running = jnp.zeros((hb_rows, LANES), jnp.float32)
        for g in range(groups):
            piece = counted[g * hb_rows:(g + 1) * hb_rows]
            pre[g] = piece[:, :LANES] + running
            running = running + piece[:, LANES:]
        for load in loads[1:4]:
            load.wait()
        every = jnp.broadcast_to(owner_ref[...], (hb_rows, LANES))
        column = jnp.transpose(every)
        smaller = jnp.where(every < column, 1.0, 0.0).astype(jnp.bfloat16)
        place = jnp.dot(smaller, ones, preferred_element_type=jnp.float32)
        local = (column % own_rows).astype(jnp.float32)
        pos_ref[0] = jnp.sum(
            jnp.where(place.astype(jnp.int32) == wide, local, 0.0), axis=0, keepdims=True
        ).astype(jnp.int32)
        chunks = jnp.floor((jnp.maximum(running - CAP, 0.0) + (CHUNK - 1)) * (1.0 / CHUNK))
        high = jnp.floor(chunks * (1.0 / 16))
        low = chunks - 16 * high
        start = 16 * jnp.dot(
            after, high.astype(jnp.bfloat16), preferred_element_type=jnp.float32
        ) + jnp.dot(after, low.astype(jnp.bfloat16), preferred_element_type=jnp.float32)
        total = start[hb_rows - 1:, :] + chunks[hb_rows - 1:, :]
        base_fixed = place * CAP
        base_rest = start * CHUNK + (fixed - CAP)
        spread(0)
        tall_sub = lax.broadcasted_iota(jnp.int32, (tall, LANES), 0)
        for g in range(groups):
            at = slice(g * LANES, (g + 1) * LANES)
            here = hot[g * hb_rows:(g + 1) * hb_rows, :].astype(jnp.float32)
            seen = pre[g]
            goal = seen + jnp.where(seen < CAP, base_fixed, base_rest)
            goal = jnp.sum(goal * here, axis=0, keepdims=True).astype(jnp.int32)
            row = jnp.sum(place * here, axis=0, keepdims=True)
            ok = g * LANES + lane < live
            goal = jnp.where(ok, goal, -1)
            left[:, at] = jnp.where(tall_sub == goal // LANES, 1.0, 0.0).astype(jnp.bfloat16)
            match = sub == goal % LANES
            digits = (
                block_ref[g:g + 1, :].astype(jnp.float32),
                (state_ref[g:g + 1, :] + 1).astype(jnp.float32),
                row,
            )
            for d, digit in enumerate(digits):
                right[d * LANES:(d + 1) * LANES, at] = jnp.where(match, digit, 0.0).astype(
                    jnp.bfloat16
                )
        table = lax.dot_general(
            left[...], right[...], (((1,), (1,)), ((), ())), preferred_element_type=jnp.float32
        ).astype(jnp.int32)
        keys = table[:, :LANES] + (table[:, LANES:2 * LANES] << 8) + (table[:, 2 * LANES:] << 16)
        keys_ref[...] = keys[:fixed // LANES]
        more_ref[:e_cap // LANES] = keys[fixed // LANES:]
        more_ref[e_cap // LANES:] = jnp.broadcast_to(total, (8, LANES)).astype(jnp.int32)
        for p in range(1, PIECES):
            spread(p)

        @pl.loop(0, hb_rows)
        def _(j):
            base_ref[j] = jnp.zeros((size, size), jnp.float32)

        for p in range(PIECES):
            for i in range(2):
                relay(p, theirs[i], i).wait_recv()
                pass_on(across, p, theirs[i]).start()
            over_y(p, across, 1).wait_recv()
            pass_on(across, p, rest).start()
        share(beside).wait_recv()
        for p in range(PIECES):
            for which in range(4):
                pass_on(beyond, p, which).wait_recv()
        for p in range(PIECES):
            for i in range(2):
                over_y(p, t, i).wait_send()
                relay(p, mine, i).wait_send()
            for which in range(4):
                pass_on(across, p, which).wait_send()
        share(t).wait_send()
        loads[4].wait()
        loads[5].wait()

    vmem = pl.BlockSpec(memory_space=pltpu.VMEM)
    dma = pltpu.SemaphoreType.DMA
    return pl.pallas_call(
        kernel,
        out_shape=(
            jax.ShapeDtypeStruct((fixed // LANES, LANES), jnp.int32),
            jax.ShapeDtypeStruct((e_cap // LANES + 8, LANES), jnp.int32),
            jax.ShapeDtypeStruct((1, 1, LANES), jnp.int32),
            jax.ShapeDtypeStruct(integrals.shape, integrals.dtype),
            jax.ShapeDtypeStruct((states + 1, size, size), densities.dtype),
            jax.ShapeDtypeStruct((hb_rows, size, size), jnp.float32),
        ),
        in_specs=[pl.BlockSpec(memory_space=pltpu.HBM)] * 7,
        out_specs=(vmem,) * 6,
        scratch_shapes=[
            pltpu.SMEM(counts.shape, jnp.int32),
            pltpu.VMEM(flat, jnp.int32),
            pltpu.VMEM(flat, jnp.int32),
            pltpu.VMEM(flat, jnp.int32),
            pltpu.VMEM((1, hb_rows), jnp.int32),
            pltpu.VMEM((groups * hb_rows, LANES), jnp.bfloat16),
            pltpu.VMEM((groups, hb_rows, LANES), jnp.float32),
            pltpu.VMEM((tall, e_cap), jnp.bfloat16),
            pltpu.VMEM((3 * LANES, e_cap), jnp.bfloat16),
            dma((7,)),
            dma((2, PIECES)), dma((2, PIECES)), dma((2, PIECES)), dma((2, PIECES)),
            dma((4, PIECES)), dma((4, PIECES)), dma, dma,
        ],
        compiler_params=pltpu.CompilerParams(
            collective_id=1, has_side_effects=True, vmem_limit_bytes=34 << 20
        ),
    )(
        *(
            pltpu.with_memory_space_constraint(x, pltpu.HBM)
            for x in (
                counts, entry_block.reshape(flat), entry_state.reshape(flat),
                entry_slot.reshape(flat),
                owner.reshape(1, hb_rows), integrals, densities,
            )
        ),
    )


def spill(keys, integrals, table, zeros):
    tall = keys.shape[0] - 8

    def kernel(keys_ref, ints, dens, zeros_ref, acc):
        del zeros_ref

        @pl.loop(0, (keys_ref[tall, 0] + UNROLL - 1) // UNROLL)
        def _(step):
            prods = []
            for u in range(UNROLL):
                base = (step * UNROLL + u) * CHUNK
                ks = [keys_ref[(base + i) >> 7, (base + i) & 127] for i in range(CHUNK)]
                lhs = jnp.concatenate([ints[k & 255] for k in ks], axis=1)
                rhs = jnp.concatenate([dens[(k >> 8) & 255] for k in ks], axis=0)
                prods.append(
                    (ks[0] >> 16, jnp.dot(lhs, rhs, preferred_element_type=jnp.float32))
                )
            for row, prod in prods:
                acc[row] += prod

    vmem = pl.BlockSpec(memory_space=pltpu.VMEM)
    return pl.pallas_call(
        kernel,
        out_shape=jax.ShapeDtypeStruct(zeros.shape, jnp.float32),
        in_specs=[pl.BlockSpec(memory_space=pltpu.SMEM), vmem, vmem, vmem],
        out_specs=vmem,
        input_output_aliases={3: 0},
        compiler_params=pltpu.CompilerParams(vmem_limit_bytes=8 << 20),
    )(keys, integrals, table, zeros)


def narrow(x):
    top = jnp.maximum(jnp.max(jnp.abs(x), axis=0, keepdims=True), SMALLEST)
    return jnp.round(x * (LEVELS / top)).astype(jnp.int32).astype(jnp.int16), top * (1.0 / LEVELS)


def widen(q, step):
    return q.astype(jnp.int32).astype(jnp.float32) * step


def exchange(keys, integrals, table, extra, pos, own_rows, n_blk):
    size = integrals.shape[-1]
    steps = min(STEPS, n_blk)
    rows = own_rows // steps
    dests = n_blk // steps
    per = own_rows // n_blk
    hb_rows = extra.shape[0]

    def kernel(keys_ref, ints, dens, base, pos_ref, out, pos_out, acc, r1, s2, r2, s3, got,
               step2, step2_in, step3, step3_in, s1_send, s1_recv, s2_send, s2_recv, t2_send,
               t2_recv, s3_send, s3_recv, t3_send, t3_recv, p_send, p_recv):
        t = lax.axis_index("tgt")
        b = lax.axis_index("blk")
        y, c = t // 2, t % 2
        sibling = y * 2 + (1 - c)
        across = (1 - y) * 2 + c
        barrier = pltpu.get_barrier_semaphore()
        pl.semaphore_signal(barrier, inc=1, device_id={"tgt": sibling}, device_id_type=MESH)
        pl.semaphore_signal(barrier, inc=1, device_id={"tgt": across}, device_id_type=MESH)
        for i in range(1, n_blk):
            pl.semaphore_signal(
                barrier, inc=1, device_id={"blk": (b + i) % n_blk}, device_id_type=MESH
            )

        def shift(i):
            return steps // 2 + (1 - 2 * (i % 2)) * ((i + 1) // 2)

        def line(i):
            return (b // dests + shift(i)) % steps

        def span(i):
            return line(i) * rows

        def first(i, far):
            side = 1 - y if far else y
            return pltpu.make_async_remote_copy(
                src_ref=acc.at[pl.ds((side * 2 + 1 - c) * own_rows + span(i), rows)],
                dst_ref=r1.at[far, pl.ds(span(i), rows)],
                send_sem=s1_send.at[far, i],
                recv_sem=s1_recv.at[far, i],
                device_id={"tgt": sibling},
                device_id_type=MESH,
            )

        def second(i):
            return pltpu.make_async_remote_copy(
                src_ref=s2.at[pl.ds(span(i), rows)],
                dst_ref=r2.at[pl.ds(span(i), rows)],
                send_sem=s2_send.at[i],
                recv_sem=s2_recv.at[i],
                device_id={"tgt": across},
                device_id_type=MESH,
            )

        def second_steps(i):
            return pltpu.make_async_remote_copy(
                src_ref=step2.at[i, pl.ds(0, rows)],
                dst_ref=step2_in.at[i, pl.ds(0, rows)],
                send_sem=t2_send.at[i],
                recv_sem=t2_recv.at[i],
                device_id={"tgt": across},
                device_id_type=MESH,
            )

        def third(dest, slot):
            return pltpu.make_async_remote_copy(
                src_ref=s3.at[pl.ds(dest * per, per)],
                dst_ref=got.at[pl.ds(slot * per, per)],
                send_sem=s3_send.at[dest],
                recv_sem=s3_recv.at[slot],
                device_id={"blk": dest},
                device_id_type=MESH,
            )

        def third_steps(dest, slot):
            return pltpu.make_async_remote_copy(
                src_ref=step3.at[dest, pl.ds(0, per)],
                dst_ref=step3_in.at[slot, pl.ds(0, per)],
                send_sem=t3_send.at[dest],
                recv_sem=t3_recv.at[slot],
                device_id={"blk": dest},
                device_id_type=MESH,
            )

        def places(dest, slot):
            return pltpu.make_async_remote_copy(
                src_ref=pos_ref.at[0],
                dst_ref=pos_out.at[slot],
                send_sem=p_send.at[dest],
                recv_sem=p_recv.at[slot],
                device_id={"blk": dest},
                device_id_type=MESH,
            )

        def multiply(i, far):
            side = 1 - y if far else y
            for core in (1 - c, c):
                for k in range(rows):
                    row = (side * 2 + core) * own_rows + span(i) + k
                    ks = []
                    for e in range(CAP):
                        at = row * CAP + e
                        ks.append(keys_ref[at // LANES, at % LANES])
                    lhs = jnp.concatenate([ints[key & 255] for key in ks], axis=1)
                    rhs = jnp.concatenate([dens[(key >> 8) & 255] for key in ks], axis=0)
                    acc[row] = base[row] + jnp.dot(lhs, rhs, preferred_element_type=jnp.float32)

        def reduce_far(i):
            for k in range(rows):
                row = span(i) + k
                q, step = narrow(acc[((1 - y) * 2 + c) * own_rows + row] + r1[1, row])
                s2[row] = q
                step2[i, k:k + 1, :] = step

        def dest_of(i, j):
            return line(i) * dests + (b % dests + j) % dests

        def reduce_near(i, own):
            for j in range(dests):
                dest = dest_of(i, j)
                for k in range(per):
                    row = dest * per + k
                    at = (b % dests + j) % dests * per + k if dests > 1 else k
                    scale = step2_in[i, pl.ds(at, 1), :]
                    total = acc[(y * 2 + c) * own_rows + row] + r1[0, row] + widen(r2[row], scale)
                    if own and j == 0:
                        out[row] = total
                    else:
                        q, step = narrow(total)
                        s3[row] = q
                        step3[dest, k:k + 1, :] = step

        def await_near(i):
            first(i, 0).wait_recv()
            second(i).wait_recv()
            second_steps(i).wait_recv()

        def send_far(i):
            second(i).start()
            second_steps(i).start()

        def send_near(i, own):
            for j in range(1 if own else 0, dests):
                dest = dest_of(i, j)
                third(dest, b).start()
                third_steps(dest, b).start()

        def finish(i, own):
            await_near(i)
            reduce_near(i, own)
            send_near(i, own)

        def open_far(i, carry):
            multiply(i, 1)

            @pl.when(i == 0)
            def _():
                pl.semaphore_wait(barrier, n_blk + 1)
                for j in range(1, n_blk):
                    places((b + j) % n_blk, b).start()
                pos_out[b] = pos_ref[0]

            first(i, 1).start()
            return carry

        def turn(i, carry):
            first(i, 1).wait_recv()
            reduce_far(i)
            send_far(i)
            multiply(i + 2, 1)
            multiply(i, 0)
            first(i + 2, 1).start()
            first(i, 0).start()

            @pl.when(i >= 1)
            def _():
                finish(i - 1, False)

            return carry

        def close(i, carry):
            first(i, 1).wait_recv()
            reduce_far(i)
            send_far(i)
            multiply(i, 0)
            first(i, 0).start()
            finish(i - 1, False)
            return carry

        lax.fori_loop(0, 2, open_far, 0)
        lax.fori_loop(0, steps - 2, turn, 0)
        lax.fori_loop(steps - 2, steps, close, 0)

        def arrive(i, carry):
            for j in range(dests):
                source = (b // dests - shift(i) + steps) % steps * dests
                source = source + (b % dests - j + dests) % dests
                third(source, source).wait_recv()
                third_steps(source, source).wait_recv()
                for k in range(per):
                    out[source * per + k] = widen(
                        got[source * per + k], step3_in[source, k:k + 1, :]
                    )
            return carry

        lax.fori_loop(0, steps // 2, arrive, 0)
        for i in range(steps - LAG, steps):
            finish(i, i == steps - 1)
        lax.fori_loop(steps // 2, steps - 1, arrive, 0)
        for j in range(1, dests):
            source = b // dests * dests + (b % dests - j + dests) % dests
            third(source, source).wait_recv()
            third_steps(source, source).wait_recv()
            for k in range(per):
                out[source * per + k] = widen(got[source * per + k], step3_in[source, k:k + 1, :])

        for i in range(steps):
            first(i, 1).wait_send()
            first(i, 0).wait_send()
            second(i).wait_send()
            second_steps(i).wait_send()
        for i in range(1, n_blk):
            peer = (b + i) % n_blk
            third(peer, b).wait_send()
            third_steps(peer, b).wait_send()
            places(peer, b).wait_send()
            places(peer, peer).wait_recv()

    vmem = pl.BlockSpec(memory_space=pltpu.VMEM)
    dma = pltpu.SemaphoreType.DMA
    block = (own_rows, size, size)
    return pl.pallas_call(
        kernel,
        out_shape=(
            jax.ShapeDtypeStruct(block, jnp.float32),
            jax.ShapeDtypeStruct((n_blk, 1, LANES), jnp.int32),
        ),
        in_specs=[pl.BlockSpec(memory_space=pltpu.SMEM)] + [vmem] * 4,
        out_specs=(vmem, vmem),
        scratch_shapes=[
            pltpu.VMEM((hb_rows, size, size), jnp.float32),
            pltpu.VMEM((2,) + block, jnp.float32),
            pltpu.VMEM(block, jnp.int16),
            pltpu.VMEM(block, jnp.int16),
            pltpu.VMEM(block, jnp.int16),
            pltpu.VMEM(block, jnp.int16),
            pltpu.VMEM((steps, 8, size), jnp.float32),
            pltpu.VMEM((steps, 8, size), jnp.float32),
            pltpu.VMEM((n_blk, 8, size), jnp.float32),
            pltpu.VMEM((n_blk, 8, size), jnp.float32),
            dma((2, steps)), dma((2, steps)),
            dma((steps,)), dma((steps,)),
            dma((steps,)), dma((steps,)),
            dma((n_blk,)), dma((n_blk,)),
            dma((n_blk,)), dma((n_blk,)),
            dma((n_blk,)), dma((n_blk,)),
        ],
        compiler_params=pltpu.CompilerParams(
            collective_id=0, has_side_effects=True, vmem_limit_bytes=22 << 20
        ),
    )(keys, integrals, table, extra, pos)


def arrange(blocks, pos, begin):
    n = blocks.shape[0]
    n_blk = pos.shape[0]
    per = n // n_blk

    def kernel(begin_ref, pos_ref, src, dst, sem):
        for s in range(n_blk):
            for k in range(per):
                pltpu.make_async_copy(
                    src.at[s * per + k], dst.at[pos_ref[s, 0, begin_ref[0] + k]], sem
                ).start()
        pltpu.make_async_copy(src, dst, sem).wait()

    smem = pl.BlockSpec(memory_space=pltpu.SMEM)
    return pl.pallas_call(
        kernel,
        out_shape=jax.ShapeDtypeStruct(blocks.shape, jnp.float32),
        in_specs=[smem, smem, pl.BlockSpec(memory_space=pl.ANY)],
        out_specs=pl.BlockSpec(memory_space=pl.ANY),
        scratch_shapes=[pltpu.SemaphoreType.DMA],
        compiler_params=pltpu.CompilerParams(vmem_limit_bytes=2 << 20),
    )(begin, pos, blocks)


def on_device(integrals, densities, entry_block, entry_state, entry_slot, counts, owner):
    hb_rows = owner.shape[0]
    n_tgt = lax.axis_size("tgt")
    n_blk = lax.axis_size("blk")
    own_rows = hb_rows // n_tgt
    t = lax.axis_index("tgt")
    b = lax.axis_index("blk")
    keys, more, pos, ints, table, zeros = route(
        entry_block, entry_state, entry_slot, counts, owner, integrals, densities, own_rows
    )
    extra = spill(more, ints, table, zeros)
    got, where = exchange(keys, ints, table, extra, pos, own_rows, n_blk)
    begin = (t * own_rows + b * (own_rows // n_blk)).reshape(1)
    return arrange(got, where, begin)


def solution(mesh):
    in_specs = (
        P(("tgt", "blk"), None, None),
        P("tgt", None, None),
        P(("tgt", "blk")),
        P(("tgt", "blk")),
        P(("tgt", "blk")),
        P(("tgt", "blk"), None),
        P("blk"),
    )
    out_specs = P(("tgt", "blk"), None, None)
    return jax.shard_map(
        on_device, mesh=mesh, in_specs=in_specs, out_specs=out_specs, check_vma=False
    )
```

```python
import jax
import jax.numpy as jnp
from jax import lax
from jax.experimental import pallas as pl
from jax.experimental.pallas import tpu as pltpu
from jax.sharding import PartitionSpec as P

CAP = 16
CHUNK = 4
UNROLL = 16
STEPS = 8
LAG = 1
PIECES = 3
LANES = 128
MESH = pl.DeviceIdType.MESH
LEVELS = 32767.0
SMALLEST = 1e-33


def route(entry_block, entry_state, entry_slot, counts, owner, integrals, densities, own_rows):
    s_group, size, _ = densities.shape
    states = s_group * lax.axis_size("tgt")
    quarter = size // 4
    cut = s_group // PIECES
    e_cap = entry_block.shape[0]
    hb_rows = owner.shape[0]
    groups = e_cap // LANES
    flat = (groups, LANES)
    fixed = hb_rows * CAP
    tall = (fixed + e_cap) // LANES

    def kernel(counts_hbm, block_hbm, state_hbm, slot_hbm, owner_hbm, int_hbm, den_hbm,
               keys_ref, more_ref, pos_ref, ints_ref, table_ref, base_ref, counts_ref, block_ref, state_ref, slot_ref, owner_ref,
               hot, pre, left, right, sems, y_send, y_recv, x_send, x_recv, c_send, c_recv,
               o_send, o_recv):
        t = lax.axis_index("tgt")
        b = lax.axis_index("blk")
        beside = (t // 2) * 2 + 1 - t % 2
        across = (1 - t // 2) * 2 + t % 2
        beyond = (1 - t // 2) * 2 + 1 - t % 2
        x, z = b % 2, b // 2 % 2
        mates = (b + 1 - 2 * x, b + 2 - 4 * z)
        mine = 2 * z + x
        theirs = (2 * z + 1 - x, 2 * (1 - z) + x)
        rest = 3 - mine

        def part(group, p, which):
            return table_ref.at[
                pl.ds(1 + group * s_group + p * cut, cut), pl.ds(which * quarter, quarter)
            ]

        def over_y(p, to, i):
            which = rest if i else mine
            return pltpu.make_async_remote_copy(
                src_ref=den_hbm.at[pl.ds(p * cut, cut), pl.ds(which * quarter, quarter)],
                dst_ref=part(to, p, which),
                send_sem=y_send.at[i, p], recv_sem=y_recv.at[i, p],
                device_id={"tgt": across}, device_id_type=MESH,
            )

        def relay(p, which, i):
            return pltpu.make_async_remote_copy(
                src_ref=part(across, p, which), dst_ref=part(across, p, which),
                send_sem=x_send.at[i, p], recv_sem=x_recv.at[i, p],
                device_id={"blk": mates[i]}, device_id_type=MESH,
            )

        def pass_on(group, p, which):
            return pltpu.make_async_remote_copy(
                src_ref=part(group, p, which), dst_ref=part(group, p, which),
                send_sem=c_send.at[which, p], recv_sem=c_recv.at[which, p],
                device_id={"tgt": beside}, device_id_type=MESH,
            )

        def share(group):
            return pltpu.make_async_remote_copy(
                src_ref=den_hbm, dst_ref=table_ref.at[pl.ds(1 + group * s_group, s_group)],
                send_sem=o_send, recv_sem=o_recv,
                device_id={"tgt": beside}, device_id_type=MESH,
            )

        def spread(p):
            over_y(p, across, 0).wait_recv()
            for i in range(2):
                relay(p, mine, i).start()
            pass_on(across, p, mine).start()

        barrier = pltpu.get_barrier_semaphore()
        for peer in ({"tgt": beside}, {"tgt": across}, {"blk": mates[0]}, {"blk": mates[1]}):
            pl.semaphore_signal(barrier, inc=1, device_id=peer, device_id_type=MESH)
        moves = (
            (slot_hbm, slot_ref), (owner_hbm, owner_ref), (block_hbm, block_ref),
            (state_hbm, state_ref), (int_hbm, ints_ref),
            (den_hbm, table_ref.at[pl.ds(1 + t * s_group, s_group)]),
            (counts_hbm, counts_ref),
        )
        loads = [
            pltpu.make_async_copy(src, dst, sems.at[i]) for i, (src, dst) in enumerate(moves)
        ]
        for load in loads:
            load.start()
        table_ref[0] = jnp.zeros((size, size), table_ref.dtype)
        pl.semaphore_wait(barrier, 4)
        for i in range(2):
            for p in range(PIECES):
                over_y(p, t, i).start()
        share(t).start()
        loads[6].wait()
        live = counts_ref[0, 0]
        for i in range(1, counts.shape[1]):
            live = live + counts_ref[0, i]
        lane = lax.broadcasted_iota(jnp.int32, (1, LANES), 1)
        sub = lax.broadcasted_iota(jnp.int32, (hb_rows, LANES), 0)
        wide = lax.broadcasted_iota(jnp.int32, (hb_rows, LANES), 1)
        loads[0].wait()
        for g in range(groups):
            ok = g * LANES + lane < live
            slot = jnp.where(ok, slot_ref[g:g + 1, :], -1)
            hot[g * hb_rows:(g + 1) * hb_rows, :] = jnp.where(
                sub == slot, 1.0, 0.0
            ).astype(jnp.bfloat16)
        before = jnp.where(sub < wide, 1.0, 0.0).astype(jnp.bfloat16)
        after = jnp.where(wide < sub, 1.0, 0.0).astype(jnp.bfloat16)
        ones = jnp.ones((LANES, LANES), jnp.bfloat16)
        counted = jnp.dot(
            hot[...], jnp.concatenate([before, ones], axis=1), preferred_element_type=jnp.float32
        )
        running = jnp.zeros((hb_rows, LANES), jnp.float32)
        for g in range(groups):
            piece = counted[g * hb_rows:(g + 1) * hb_rows]
            pre[g] = piece[:, :LANES] + running
            running = running + piece[:, LANES:]
        for load in loads[1:4]:
            load.wait()
        every = jnp.broadcast_to(owner_ref[...], (hb_rows, LANES))
        column = jnp.transpose(every)
        smaller = jnp.where(every < column, 1.0, 0.0).astype(jnp.bfloat16)
        place = jnp.dot(smaller, ones, preferred_element_type=jnp.float32)
        local = (column % own_rows).astype(jnp.float32)
        pos_ref[0] = jnp.sum(
            jnp.where(place.astype(jnp.int32) == wide, local, 0.0), axis=0, keepdims=True
        ).astype(jnp.int32)
        chunks = jnp.floor((jnp.maximum(running - CAP, 0.0) + (CHUNK - 1)) * (1.0 / CHUNK))
        high = jnp.floor(chunks * (1.0 / 16))
        low = chunks - 16 * high
        start = 16 * jnp.dot(
            after, high.astype(jnp.bfloat16), preferred_element_type=jnp.float32
        ) + jnp.dot(after, low.astype(jnp.bfloat16), preferred_element_type=jnp.float32)
        total = start[hb_rows - 1:, :] + chunks[hb_rows - 1:, :]
        base_fixed = place * CAP
        base_rest = start * CHUNK + (fixed - CAP)
        spread(0)
        tall_sub = lax.broadcasted_iota(jnp.int32, (tall, LANES), 0)
        for g in range(groups):
            at = slice(g * LANES, (g + 1) * LANES)
            here = hot[g * hb_rows:(g + 1) * hb_rows, :].astype(jnp.float32)
            seen = pre[g]
            goal = seen + jnp.where(seen < CAP, base_fixed, base_rest)
            goal = jnp.sum(goal * here, axis=0, keepdims=True).astype(jnp.int32)
            row = jnp.sum(place * here, axis=0, keepdims=True)
            ok = g * LANES + lane < live
            goal = jnp.where(ok, goal, -1)
            left[:, at] = jnp.where(tall_sub == goal // LANES, 1.0, 0.0).astype(jnp.bfloat16)
            match = sub == goal % LANES
            digits = (
                block_ref[g:g + 1, :].astype(jnp.float32),
                (state_ref[g:g + 1, :] + 1).astype(jnp.float32),
                row,
            )
            for d, digit in enumerate(digits):
                right[d * LANES:(d + 1) * LANES, at] = jnp.where(match, digit, 0.0).astype(
                    jnp.bfloat16
                )
        table = lax.dot_general(
            left[...], right[...], (((1,), (1,)), ((), ())), preferred_element_type=jnp.float32
        ).astype(jnp.int32)
        keys = table[:, :LANES] + (table[:, LANES:2 * LANES] << 8) + (table[:, 2 * LANES:] << 16)
        keys_ref[...] = keys[:fixed // LANES]
        more_ref[:e_cap // LANES] = keys[fixed // LANES:]
        more_ref[e_cap // LANES:] = jnp.broadcast_to(total, (8, LANES)).astype(jnp.int32)
        for p in range(1, PIECES):
            spread(p)

        @pl.loop(0, hb_rows)
        def _(j):
            base_ref[j] = jnp.zeros((size, size), jnp.float32)

        for p in range(PIECES):
            for i in range(2):
                relay(p, theirs[i], i).wait_recv()
                pass_on(across, p, theirs[i]).start()
            over_y(p, across, 1).wait_recv()
            pass_on(across, p, rest).start()
        share(beside).wait_recv()
        for p in range(PIECES):
            for which in range(4):
                pass_on(beyond, p, which).wait_recv()
        for p in range(PIECES):
            for i in range(2):
                over_y(p, t, i).wait_send()
                relay(p, mine, i).wait_send()
            for which in range(4):
                pass_on(across, p, which).wait_send()
        share(t).wait_send()
        loads[4].wait()
        loads[5].wait()

    vmem = pl.BlockSpec(memory_space=pltpu.VMEM)
    dma = pltpu.SemaphoreType.DMA
    return pl.pallas_call(
        kernel,
        out_shape=(
            jax.ShapeDtypeStruct((fixed // LANES, LANES), jnp.int32),
            jax.ShapeDtypeStruct((e_cap // LANES + 8, LANES), jnp.int32),
            jax.ShapeDtypeStruct((1, 1, LANES), jnp.int32),
            jax.ShapeDtypeStruct(integrals.shape, integrals.dtype),
            jax.ShapeDtypeStruct((states + 1, size, size), densities.dtype),
            jax.ShapeDtypeStruct((hb_rows, size, size), jnp.float32),
        ),
        in_specs=[pl.BlockSpec(memory_space=pltpu.HBM)] * 7,
        out_specs=(vmem,) * 6,
        scratch_shapes=[
            pltpu.SMEM(counts.shape, jnp.int32),
            pltpu.VMEM(flat, jnp.int32),
            pltpu.VMEM(flat, jnp.int32),
            pltpu.VMEM(flat, jnp.int32),
            pltpu.VMEM((1, hb_rows), jnp.int32),
            pltpu.VMEM((groups * hb_rows, LANES), jnp.bfloat16),
            pltpu.VMEM((groups, hb_rows, LANES), jnp.float32),
            pltpu.VMEM((tall, e_cap), jnp.bfloat16),
            pltpu.VMEM((3 * LANES, e_cap), jnp.bfloat16),
            dma((7,)),
            dma((2, PIECES)), dma((2, PIECES)), dma((2, PIECES)), dma((2, PIECES)),
            dma((4, PIECES)), dma((4, PIECES)), dma, dma,
        ],
        compiler_params=pltpu.CompilerParams(
            collective_id=1, has_side_effects=True, vmem_limit_bytes=34 << 20
        ),
    )(
        *(
            pltpu.with_memory_space_constraint(x, pltpu.HBM)
            for x in (
                counts, entry_block.reshape(flat), entry_state.reshape(flat),
                entry_slot.reshape(flat),
                owner.reshape(1, hb_rows), integrals, densities,
            )
        ),
    )


def spill(keys, integrals, table, zeros):
    tall = keys.shape[0] - 8

    def kernel(keys_ref, ints, dens, zeros_ref, acc):
        del zeros_ref

        @pl.loop(0, (keys_ref[tall, 0] + UNROLL - 1) // UNROLL)
        def _(step):
            prods = []
            for u in range(UNROLL):
                base = (step * UNROLL + u) * CHUNK
                ks = [keys_ref[(base + i) >> 7, (base + i) & 127] for i in range(CHUNK)]
                lhs = jnp.concatenate([ints[k & 255] for k in ks], axis=1)
                rhs = jnp.concatenate([dens[(k >> 8) & 255] for k in ks], axis=0)
                prods.append(
                    (ks[0] >> 16, jnp.dot(lhs, rhs, preferred_element_type=jnp.float32))
                )
            for row, prod in prods:
                acc[row] += prod

    vmem = pl.BlockSpec(memory_space=pltpu.VMEM)
    return pl.pallas_call(
        kernel,
        out_shape=jax.ShapeDtypeStruct(zeros.shape, jnp.float32),
        in_specs=[pl.BlockSpec(memory_space=pltpu.SMEM), vmem, vmem, vmem],
        out_specs=vmem,
        input_output_aliases={3: 0},
        compiler_params=pltpu.CompilerParams(vmem_limit_bytes=8 << 20),
    )(keys, integrals, table, zeros)


def narrow(x):
    top = jnp.maximum(jnp.max(jnp.abs(x), axis=0, keepdims=True), SMALLEST)
    return jnp.round(x * (LEVELS / top)).astype(jnp.int32).astype(jnp.int16), top * (1.0 / LEVELS)


def widen(q, step):
    return q.astype(jnp.int32).astype(jnp.float32) * step


def exchange(keys, integrals, table, extra, pos, own_rows, n_blk):
    size = integrals.shape[-1]
    steps = min(STEPS, n_blk)
    rows = own_rows // steps
    dests = n_blk // steps
    per = own_rows // n_blk
    hb_rows = extra.shape[0]

    def kernel(keys_ref, ints, dens, base, pos_ref, out, pos_out, acc, r1, s2, r2, s3, got,
               step2, step2_in, step3, step3_in, s1_send, s1_recv, s2_send, s2_recv, t2_send,
               t2_recv, s3_send, s3_recv, t3_send, t3_recv, p_send, p_recv):
        t = lax.axis_index("tgt")
        b = lax.axis_index("blk")
        y, c = t // 2, t % 2
        sibling = y * 2 + (1 - c)
        across = (1 - y) * 2 + c
        barrier = pltpu.get_barrier_semaphore()
        pl.semaphore_signal(barrier, inc=1, device_id={"tgt": sibling}, device_id_type=MESH)
        pl.semaphore_signal(barrier, inc=1, device_id={"tgt": across}, device_id_type=MESH)
        for i in range(1, n_blk):
            pl.semaphore_signal(
                barrier, inc=1, device_id={"blk": (b + i) % n_blk}, device_id_type=MESH
            )

        def shift(i):
            return steps // 2 + (1 - 2 * (i % 2)) * ((i + 1) // 2)

        def line(i):
            return (b // dests + shift(i)) % steps

        def span(i):
            return line(i) * rows

        def first(i, far):
            side = 1 - y if far else y
            return pltpu.make_async_remote_copy(
                src_ref=acc.at[pl.ds((side * 2 + 1 - c) * own_rows + span(i), rows)],
                dst_ref=r1.at[far, pl.ds(span(i), rows)],
                send_sem=s1_send.at[far, i],
                recv_sem=s1_recv.at[far, i],
                device_id={"tgt": sibling},
                device_id_type=MESH,
            )

        def second(i):
            return pltpu.make_async_remote_copy(
                src_ref=s2.at[pl.ds(span(i), rows)],
                dst_ref=r2.at[pl.ds(span(i), rows)],
                send_sem=s2_send.at[i],
                recv_sem=s2_recv.at[i],
                device_id={"tgt": across},
                device_id_type=MESH,
            )

        def second_steps(i):
            return pltpu.make_async_remote_copy(
                src_ref=step2.at[i, pl.ds(0, rows)],
                dst_ref=step2_in.at[i, pl.ds(0, rows)],
                send_sem=t2_send.at[i],
                recv_sem=t2_recv.at[i],
                device_id={"tgt": across},
                device_id_type=MESH,
            )

        def third(dest, slot):
            return pltpu.make_async_remote_copy(
                src_ref=s3.at[pl.ds(dest * per, per)],
                dst_ref=got.at[pl.ds(slot * per, per)],
                send_sem=s3_send.at[dest],
                recv_sem=s3_recv.at[slot],
                device_id={"blk": dest},
                device_id_type=MESH,
            )

        def third_steps(dest, slot):
            return pltpu.make_async_remote_copy(
                src_ref=step3.at[dest, pl.ds(0, per)],
                dst_ref=step3_in.at[slot, pl.ds(0, per)],
                send_sem=t3_send.at[dest],
                recv_sem=t3_recv.at[slot],
                device_id={"blk": dest},
                device_id_type=MESH,
            )

        def places(dest, slot):
            return pltpu.make_async_remote_copy(
                src_ref=pos_ref.at[0],
                dst_ref=pos_out.at[slot],
                send_sem=p_send.at[dest],
                recv_sem=p_recv.at[slot],
                device_id={"blk": dest},
                device_id_type=MESH,
            )

        def multiply(i, far):
            side = 1 - y if far else y
            for core in (1 - c, c):
                for k in range(rows):
                    row = (side * 2 + core) * own_rows + span(i) + k
                    ks = []
                    for e in range(CAP):
                        at = row * CAP + e
                        ks.append(keys_ref[at // LANES, at % LANES])
                    lhs = jnp.concatenate([ints[key & 255] for key in ks], axis=1)
                    rhs = jnp.concatenate([dens[(key >> 8) & 255] for key in ks], axis=0)
                    acc[row] = base[row] + jnp.dot(lhs, rhs, preferred_element_type=jnp.float32)

        def reduce_far(i):
            for k in range(rows):
                row = span(i) + k
                q, step = narrow(acc[((1 - y) * 2 + c) * own_rows + row] + r1[1, row])
                s2[row] = q
                step2[i, k:k + 1, :] = step

        def dest_of(i, j):
            return line(i) * dests + (b % dests + j) % dests

        def reduce_near(i, own):
            for j in range(dests):
                dest = dest_of(i, j)
                for k in range(per):
                    row = dest * per + k
                    at = (b % dests + j) % dests * per + k if dests > 1 else k
                    scale = step2_in[i, pl.ds(at, 1), :]
                    total = acc[(y * 2 + c) * own_rows + row] + r1[0, row] + widen(r2[row], scale)
                    if own and j == 0:
                        out[row] = total
                    else:
                        q, step = narrow(total)
                        s3[row] = q
                        step3[dest, k:k + 1, :] = step

        def await_near(i):
            first(i, 0).wait_recv()
            second(i).wait_recv()
            second_steps(i).wait_recv()

        def send_far(i):
            second(i).start()
            second_steps(i).start()

        def send_near(i, own):
            for j in range(1 if own else 0, dests):
                dest = dest_of(i, j)
                third(dest, b).start()
                third_steps(dest, b).start()

        multiply(0, 1)
        pl.semaphore_wait(barrier, n_blk + 1)
        first(0, 1).start()
        for i in range(1, n_blk):
            places((b + i) % n_blk, b).start()
        pos_out[b] = pos_ref[0]

        def finish(i, own):
            await_near(i)
            reduce_near(i, own)
            send_near(i, own)

        def turn(i, carry):
            @pl.when(i + 1 < steps)
            def _():
                multiply(i + 1, 1)
                first(i + 1, 1).start()

            first(i, 1).wait_recv()
            reduce_far(i)
            send_far(i)
            multiply(i, 0)
            first(i, 0).start()

            @pl.when(i >= LAG)
            def _():
                finish(i - LAG, False)

            return carry

        lax.fori_loop(0, steps, turn, 0)
        def arrive(i, carry):
            for j in range(dests):
                source = (b // dests - shift(i) + steps) % steps * dests
                source = source + (b % dests - j + dests) % dests
                third(source, source).wait_recv()
                third_steps(source, source).wait_recv()
                for k in range(per):
                    out[source * per + k] = widen(
                        got[source * per + k], step3_in[source, k:k + 1, :]
                    )
            return carry

        lax.fori_loop(0, steps // 2, arrive, 0)
        for i in range(steps - LAG, steps):
            finish(i, i == steps - 1)
        lax.fori_loop(steps // 2, steps - 1, arrive, 0)
        for j in range(1, dests):
            source = b // dests * dests + (b % dests - j + dests) % dests
            third(source, source).wait_recv()
            third_steps(source, source).wait_recv()
            for k in range(per):
                out[source * per + k] = widen(got[source * per + k], step3_in[source, k:k + 1, :])

        for i in range(steps):
            first(i, 1).wait_send()
            first(i, 0).wait_send()
            second(i).wait_send()
            second_steps(i).wait_send()
        for i in range(1, n_blk):
            peer = (b + i) % n_blk
            third(peer, b).wait_send()
            third_steps(peer, b).wait_send()
            places(peer, b).wait_send()
            places(peer, peer).wait_recv()

    vmem = pl.BlockSpec(memory_space=pltpu.VMEM)
    dma = pltpu.SemaphoreType.DMA
    block = (own_rows, size, size)
    return pl.pallas_call(
        kernel,
        out_shape=(
            jax.ShapeDtypeStruct(block, jnp.float32),
            jax.ShapeDtypeStruct((n_blk, 1, LANES), jnp.int32),
        ),
        in_specs=[pl.BlockSpec(memory_space=pltpu.SMEM)] + [vmem] * 4,
        out_specs=(vmem, vmem),
        scratch_shapes=[
            pltpu.VMEM((hb_rows, size, size), jnp.float32),
            pltpu.VMEM((2,) + block, jnp.float32),
            pltpu.VMEM(block, jnp.int16),
            pltpu.VMEM(block, jnp.int16),
            pltpu.VMEM(block, jnp.int16),
            pltpu.VMEM(block, jnp.int16),
            pltpu.VMEM((steps, 8, size), jnp.float32),
            pltpu.VMEM((steps, 8, size), jnp.float32),
            pltpu.VMEM((n_blk, 8, size), jnp.float32),
            pltpu.VMEM((n_blk, 8, size), jnp.float32),
            dma((2, steps)), dma((2, steps)),
            dma((steps,)), dma((steps,)),
            dma((steps,)), dma((steps,)),
            dma((n_blk,)), dma((n_blk,)),
            dma((n_blk,)), dma((n_blk,)),
            dma((n_blk,)), dma((n_blk,)),
        ],
        compiler_params=pltpu.CompilerParams(
            collective_id=0, has_side_effects=True, vmem_limit_bytes=22 << 20
        ),
    )(keys, integrals, table, extra, pos)


def arrange(blocks, pos, begin):
    n = blocks.shape[0]
    n_blk = pos.shape[0]
    per = n // n_blk

    def kernel(begin_ref, pos_ref, src, dst, sem):
        for s in range(n_blk):
            for k in range(per):
                pltpu.make_async_copy(
                    src.at[s * per + k], dst.at[pos_ref[s, 0, begin_ref[0] + k]], sem
                ).start()
        pltpu.make_async_copy(src, dst, sem).wait()

    smem = pl.BlockSpec(memory_space=pltpu.SMEM)
    return pl.pallas_call(
        kernel,
        out_shape=jax.ShapeDtypeStruct(blocks.shape, jnp.float32),
        in_specs=[smem, smem, pl.BlockSpec(memory_space=pl.ANY)],
        out_specs=pl.BlockSpec(memory_space=pl.ANY),
        scratch_shapes=[pltpu.SemaphoreType.DMA],
        compiler_params=pltpu.CompilerParams(vmem_limit_bytes=2 << 20),
    )(begin, pos, blocks)


def on_device(integrals, densities, entry_block, entry_state, entry_slot, counts, owner):
    hb_rows = owner.shape[0]
    n_tgt = lax.axis_size("tgt")
    n_blk = lax.axis_size("blk")
    own_rows = hb_rows // n_tgt
    t = lax.axis_index("tgt")
    b = lax.axis_index("blk")
    keys, more, pos, ints, table, zeros = route(
        entry_block, entry_state, entry_slot, counts, owner, integrals, densities, own_rows
    )
    extra = spill(more, ints, table, zeros)
    got, where = exchange(keys, ints, table, extra, pos, own_rows, n_blk)
    begin = (t * own_rows + b * (own_rows // n_blk)).reshape(1)
    return arrange(got, where, begin)


def solution(mesh):
    in_specs = (
        P(("tgt", "blk"), None, None),
        P("tgt", None, None),
        P(("tgt", "blk")),
        P(("tgt", "blk")),
        P(("tgt", "blk")),
        P(("tgt", "blk"), None),
        P("blk"),
    )
    out_specs = P(("tgt", "blk"), None, None)
    return jax.shard_map(
        on_device, mesh=mesh, in_specs=in_specs, out_specs=out_specs, check_vma=False
    )
```
